512 devices in a mesh: section: 16 (over z, x_hi), dp: 32 (over y, x_lo, core).
Axes of the slice: x: 4 (x_hi: 2, x_lo: 2; x = x_hi * 2 + x_lo), y: 8, z: 8, core: 2. Of those that a mesh axis runs over, the one named last changes fastest.
Arguments:
- pending_predecessor_pair: float32 [16, 2, 32, 16, 16, 512], P('section', None, 'dp'), may hold values from -6 to 6
- incoming_stem_images: float32 [3, 32, 16, 16, 512], P(None, 'dp'), may hold values from -6 to 6
- spatial_filter_entries: float32 [16, 4, 9, 512], P('section', None, None, 'dp'), may hold values from -2 to 2
- mixing_matrix_entries: float32 [16, 4, 512, 512], P('section', None, 'dp'), may hold values from -0.25 to 0.25
Outputs:
- emitted: float32 [16, 4, 32, 16, 16, 512], P('section', None, 'dp')
The draws below stay inside these ranges and needn't reach their ends.
All inputs are finite; a program needn't handle non-finite values.
Results may differ from the reference program's by a relative error of at most 0.00015.
Values sent between devices are 32-bit elements; how exact they have to be, the bound alone decides.
A program may use at most 64 MiB of HBM per device.

```python
import jax
import jax.numpy as jnp
from jax import lax

FILTER_NUMBER = 512
GRID_EXTENT = 16
TICKS = 4
CASCADE_LENGTH = 16
IMAGE_GROUP = 32


def levels(rng, extent, split, low, top_value):
    def one(dim, shards_of):
        steps = jax.random.uniform(jax.random.fold_in(jax.random.fold_in(rng, 6), dim), (shards_of,), jnp.float32, low / len(split), top_value / len(split))
        return jnp.repeat(jnp.exp(steps), extent[dim] // shards_of).reshape((-1,) + (1,) * (len(extent) - dim - 1))

    loudness = one(*split[0])
    for cut in split[1:]:
        loudness = loudness * one(*cut)
    return loudness


def normal_values(stream_key, dims, width, limit, cuts=(), dtype=jnp.bfloat16):
    loudness = levels(stream_key, dims, cuts, -0.22, 0.18) if cuts else 1.0
    array = jax.random.normal(stream_key, dims, jnp.float32) * width * loudness
    return jnp.minimum(jnp.maximum(array, -limit), limit).astype(dtype)


def setup_inputs(seed: int = 0) -> dict:
    seeds = jax.random.split(jax.random.key(seed), 5)
    return {
        "pending_predecessor_pair": normal_values(seeds[0], (CASCADE_LENGTH, 2, IMAGE_GROUP, GRID_EXTENT, GRID_EXTENT, FILTER_NUMBER), 1.0, 6.0, ((0, 16), (2, 32)), jnp.float32),
        "incoming_stem_images": normal_values(seeds[1], (TICKS - 1, IMAGE_GROUP, GRID_EXTENT, GRID_EXTENT, FILTER_NUMBER), 1.0, 6.0, ((1, 32),), jnp.float32),
        "spatial_filter_entries": normal_values(seeds[2], (CASCADE_LENGTH, 4, 9, FILTER_NUMBER), 0.333, 2.0, ((0, 16), (3, 32)), jnp.float32),
        "mixing_matrix_entries": normal_values(seeds[3], (CASCADE_LENGTH, 4, FILTER_NUMBER, FILTER_NUMBER), FILTER_NUMBER ** -0.5, 0.25, ((0, 16), (2, 32)), jnp.float32),
    }


def depthwise(source, tap_table):
    side = source.shape[1]
    padded = jnp.pad(source, ((0, 0), (1, 1), (1, 1), (0, 0)))
    running = jnp.zeros(source.shape, jnp.float32)
    for row_off in range(3):
        for col_off in range(3):
            running = running + padded[:, row_off:row_off + side, col_off:col_off + side, :] * tap_table[3 * row_off + col_off]
    return running


def separable(source, tap_table, kernel):
    mixed_in = depthwise(jnp.maximum(source, 0.0), tap_table)
    flattened = mixed_in.reshape(-1, mixed_in.shape[-1])
    result = jnp.dot(flattened, kernel, precision=lax.Precision.HIGHEST, preferred_element_type=jnp.float32)
    return result.reshape(source.shape)


def amoeba_cell(operands):
    prior_carry_output, current_carry_output, tap_table, kernels = operands
    sum_one = separable(current_carry_output, tap_table[0], kernels[0]) + separable(prior_carry_output, tap_table[1], kernels[1])
    sum_two = separable(sum_one, tap_table[2], kernels[2]) + current_carry_output
    return separable(sum_two, tap_table[3], kernels[3]) + sum_one


def reference(pending_predecessor_pair, incoming_stem_images, spatial_filter_entries, mixing_matrix_entries):
    prior_carry_output = pending_predecessor_pair[:, 0]
    current_carry_output = pending_predecessor_pair[:, 1]
    history = []
    for tick in range(TICKS):
        output = lax.map(amoeba_cell, (prior_carry_output, current_carry_output, spatial_filter_entries, mixing_matrix_entries))
        history.append(output)
        if tick < TICKS - 1:
            entering = incoming_stem_images[tick][None]
            prior_carry_output = jnp.concatenate([entering, current_carry_output[:-1]], axis=0)
            current_carry_output = jnp.concatenate([entering, output[:-1]], axis=0)
    return jnp.stack(history, axis=1)
```

```python
import functools

import jax
import jax.numpy as jnp
from jax import lax
from jax.experimental import pallas as pl
from jax.experimental.pallas import tpu as pltpu
from jax.sharding import PartitionSpec as P

MESH = pl.DeviceIdType.MESH
F32, BF16 = jnp.float32, jnp.bfloat16
GRID = 16
PIX = GRID * GRID
TICKS = 4
ROWS = 16
OWN, PAIR, LATE = 0, 1, 2


def kernel(S, Y, C, pend, stem, blk, out, G, W3, A3, B3, taps, NEW, EAR, OUT, first, second,
           lsem, ssem, fsem, bsem, xssem, xsem, cssem, csem, nssem, nrsem, essem, ersem, osem):
    D = Y * 4
    T = C // 128
    EARLY, ALL = 4 * T + 1, 8 * T + 1
    KC = C // 2
    half = Y // 2
    sec, dp = lax.axis_index("section"), lax.axis_index("dp")
    y, xl, core = dp // 4, lax.rem(dp // 2, 2), lax.rem(dp, 2)
    yup, ydn = lax.rem(dp + 4, D), lax.rem(dp + D - 4, D)
    xpair, cpair = dp + 2 - 4 * xl, dp + 1 - 2 * core
    here = lambda d: {"section": sec, "dp": d}
    at = lambda s: {"section": s, "dp": dp}
    nxt, nxt2 = lax.rem(sec + 1, S), lax.rem(sec + 2, S)
    prv, prv2 = lax.rem(sec + S - 1, S), lax.rem(sec + S - 2, S)

    local = [
        pltpu.make_async_copy(blk, G.at[core, y, xl], lsem.at[0]),
        pltpu.make_async_copy(pend.at[0], EAR.at[0], lsem.at[1]),
        pltpu.make_async_copy(pend.at[1], NEW.at[0], lsem.at[2]),
    ]
    for c in local:
        c.start()
    stems_new = [pltpu.make_async_copy(stem.at[t - 1], NEW.at[t], lsem.at[2 + t]) for t in (1, 2, 3)]
    stems_ear = [pltpu.make_async_copy(stem.at[t - 1], EAR.at[t], lsem.at[5 + t]) for t in (1, 2, 3)]
    stems_one = [pltpu.make_async_copy(stem.at[t - 2], EAR.at[t], lsem.at[5 + t]) for t in (2, 3)]

    @pl.when(sec == 0)
    def _():
        for c in stems_new + stems_ear:
            c.start()

    @pl.when(sec == 1)
    def _():
        for c in stems_one:
            c.start()

    barrier = pltpu.get_barrier_semaphore()
    for d in (here(yup), here(ydn), here(xpair), here(cpair), at(nxt), at(prv), at(nxt2), at(prv2)):
        pl.semaphore_signal(barrier, inc=1, device_id=d, device_id_type=MESH)
    pl.semaphore_wait(barrier, 8)
    local[0].wait()

    sent = []

    def remote(src, dst, s, r, dev):
        return pltpu.make_async_remote_copy(src_ref=src, dst_ref=dst, send_sem=s, recv_sem=r,
                                            device_id=dev, device_id_type=MESH)

    def send(c):
        c.start()
        sent.append(c)

    def piece(cc, yy, xx, late):
        lo, n = (EARLY, ALL - EARLY) if late else (0, EARLY)
        return G.at[cc, yy, xx, pl.ds(lo, n)]

    def ring(way, stream, k):
        yy = lax.rem(y + Y - (k - 1), Y) if way == 0 else lax.rem(y + (k - 1), Y)
        xx = 1 - xl if stream == PAIR else xl
        p = piece(core, yy, xx, stream == LATE)
        sems = fsem if way == 0 else bsem
        return remote(p, p, ssem.at[way, stream, k - 1], sems.at[stream, k - 1], here(yup if way == 0 else ydn))

    def carried(way, stream, k):
        if k < half:
            return True
        return k == half and (way == 1 if stream == PAIR else way == 0)

    def arrived(way, stream, k):
        yy = lax.rem(y + Y - k, Y) if way == 0 else lax.rem(y + k, Y)
        xx = 1 - xl if stream == PAIR else xl
        p = piece(core, yy, xx, stream == LATE)
        sems = fsem if way == 0 else bsem
        remote(p, p, ssem.at[way, stream, k - 1], sems.at[stream, k - 1], here(ydn)).wait_recv()
        return yy, xx

    def slot(way, k):
        return 0 if k == 0 else (k if way == 0 else Y - k)

    def cross(way, k):
        yy = lax.rem(y + Y - k, Y) if way == 0 else lax.rem(y + k, Y)
        p = piece(core, yy, xl, True)
        n = slot(way, k)
        return remote(p, p, xssem.at[n], xsem.at[n], here(xpair))

    def crossed(way, k):
        yy = lax.rem(y + Y - k, Y) if way == 0 else lax.rem(y + k, Y)
        p = piece(core, yy, 1 - xl, True)
        n = slot(way, k)
        remote(p, p, xssem.at[n], xsem.at[n], here(xpair)).wait_recv()
        return yy, 1 - xl

    def share(yy, xx, late, way, k, pair):
        n = (2 if pair else 0) + (1 if late else 0)
        p = piece(core, yy, xx, late)
        send(remote(p, p, cssem.at[n, slot(way, k)], csem.at[n, slot(way, k)], here(cpair)))

    def shared(yy, xx, late, way, k, pair):
        n = (2 if pair else 0) + (1 if late else 0)
        p = piece(1 - core, yy, xx, late)
        remote(p, p, cssem.at[n, slot(way, k)], csem.at[n, slot(way, k)], here(cpair)).wait_recv()

    def split(cc, yy, xx, late):
        row = pl.multiple_of(((yy * 2 + xx) * 2 + cc) * ROWS, ROWS)
        base = EARLY if late else 0

        def step(m, carry):
            b = (2 if late else 0) + m
            for j in range(T):
                w = jnp.concatenate([G[cc, yy, xx, base + m * 2 * T + j], G[cc, yy, xx, base + m * 2 * T + T + j]], 0)
                hi = w.astype(BF16)
                lo = (w - hi.astype(F32)).astype(BF16)
                lanes = slice(128 * j, 128 * j + 128)
                W3[b, pl.ds(row, ROWS), lanes] = hi
                W3[b, pl.ds(pl.multiple_of(C + row, ROWS), ROWS), lanes] = hi
                W3[b, pl.ds(pl.multiple_of(2 * C + row, ROWS), ROWS), lanes] = lo
            return carry

        lax.fori_loop(0, 2, step, 0)

    own = piece(core, y, xl, False)
    send(remote(own, own, xssem.at[Y], xsem.at[Y], here(xpair)))
    for stream in (OWN, LATE):
        for way in (0, 1):
            if carried(way, stream, 1):
                send(ring(way, stream, 1))
    send(cross(0, 0))
    share(y, xl, False, 0, 0, False)
    share(y, xl, True, 0, 0, False)

    old_copy = remote(pend.at[1], EAR.at[1], essem.at[1], ersem.at[1], at(nxt))

    split(core, y, xl, False)
    split(core, y, xl, True)
    other = piece(core, y, 1 - xl, False)
    remote(other, other, xssem.at[Y], xsem.at[Y], here(xpair)).wait_recv()
    for way in (0, 1):
        if carried(way, PAIR, 1):
            send(ring(way, PAIR, 1))
    share(y, 1 - xl, False, 0, 0, True)
    split(core, y, 1 - xl, False)

    def tail(ways, k):
        for way in ways:
            yy, xx = crossed(way, k)
            share(yy, xx, True, way, k, True)
            split(core, yy, xx, True)
        for way in ways:
            yy = lax.rem(y + Y - k, Y) if way == 0 else lax.rem(y + k, Y)
            for pair in (False, True):
                xx = 1 - xl if pair else xl
                for late in (False, True):
                    shared(yy, xx, late, way, k, pair)
                    split(1 - core, yy, xx, late)

    for k in range(1, half + 1):
        got = []
        for stream in (LATE, OWN, PAIR):
            for way in (0, 1):
                if not carried(way, stream, k):
                    continue
                yy, xx = arrived(way, stream, k)
                if carried(way, stream, k + 1):
                    send(ring(way, stream, k + 1))
                late = stream == LATE
                w = 0 if k == half else way
                if late:
                    send(cross(w, k))
                share(yy, xx, late, w, k, stream == PAIR)
                got.append((yy, xx, late))
        if k == half:
            @pl.when(sec < S - 1)
            def _():
                old_copy.start()
        for yy, xx, late in got:
            split(core, yy, xx, late)
        tail((0,) if k == 1 else (0, 1), k - 1)
    tail((0,), half)

    lane = lax.broadcasted_iota(jnp.int32, (8, 128), 1) // ROWS

    def gather_taps(g, carry):
        lanes = pl.ds(pl.multiple_of(g * 128, 128), 128)
        tiles = [G[e % 2, 2 * g + e // 4, (e // 2) % 2, EARLY - 1] for e in range(8)]
        for q in range(8):
            row = jnp.zeros((8, 128), F32)
            for e in range(8):
                shift = ((e - q) % 8) * ROWS
                moved = pltpu.roll(tiles[e], shift, 1) if shift else tiles[e]
                row = jnp.where(lane == e, moved, row)
            taps[q, :, lanes] = row
        return carry

    lax.fori_loop(0, T, gather_taps, 0)

    for c in local[1:]:
        c.wait()

    @pl.when(sec == 0)
    def _():
        for c in stems_new + stems_ear:
            c.wait()

    @pl.when(sec == 1)
    def _():
        for c in stems_one:
            c.wait()

    def tap(b, t, kc):
        n = 9 * b + t
        return taps[n % 8, n // 8:n // 8 + 1, kc * KC:(kc + 1) * KC].reshape(1, 1, KC)

    col = lax.broadcasted_iota(jnp.int32, (1, GRID, KC), 1)

    def depthwise(v, b, kc, acts):
        v = jnp.maximum(v.reshape(GRID, GRID, KC), 0.0)
        left, right = pltpu.roll(v, 1, 1), pltpu.roll(v, GRID - 1, 1)
        rows = []
        for i in range(3):
            kl = jnp.where(col == 0, 0.0, jnp.broadcast_to(tap(b, 3 * i, kc), (1, GRID, KC)))
            kr = jnp.where(col == GRID - 1, 0.0, jnp.broadcast_to(tap(b, 3 * i + 2, kc), (1, GRID, KC)))
            rows.append(left * kl + v * tap(b, 3 * i + 1, kc) + right * kr)
        zero = jnp.zeros((1, GRID, KC), F32)
        total = (jnp.concatenate([zero, rows[0][:GRID - 1]], 0) + rows[1]
                 + jnp.concatenate([rows[2][1:], zero], 0)).reshape(PIX, KC)
        hi = total.astype(BF16)
        lo = (total - hi.astype(F32)).astype(BF16)
        acts[:, kc * KC:(kc + 1) * KC] = hi
        acts[:, C + kc * KC:C + (kc + 1) * KC] = lo
        acts[:, 2 * C + kc * KC:2 * C + (kc + 1) * KC] = hi

    def product(acts, b, nc):
        return jnp.dot(acts[...], W3[b, :, nc * KC:(nc + 1) * KC], preferred_element_type=F32)

    part = lambda nc: slice(nc * KC, (nc + 1) * KC)
    span = lambda nc: pl.ds(nc * KC, KC)

    def new_copy(t, nc):
        return remote(OUT.at[t, :, span(nc)], NEW.at[t + 1, :, span(nc)], nssem.at[t, nc], nrsem.at[t + 1, nc], at(nxt))

    def ear_copy(t):
        return remote(OUT.at[t], EAR.at[t + 2], essem.at[t + 2], ersem.at[t + 2], at(nxt2))

    def out_copy(t):
        return pltpu.make_async_copy(OUT.at[t], out.at[t], osem.at[t])

    def tick(t, carry):
        @pl.when(((t == 1) & (sec > 0)) | ((t > 1) & (sec > 1)))
        def _():
            remote(EAR.at[t], EAR.at[t], essem.at[t], ersem.at[t], at(prv)).wait_recv()

        for kc in (0, 1):
            depthwise(EAR[t, :, part(kc)], 1, kc, B3)
        for nc in (0, 1):
            first[:, part(nc)] = product(B3, 1, nc)
        for kc in (0, 1):
            @pl.when((t > 0) & (sec > 0))
            def _():
                remote(NEW.at[t, :, span(kc)], NEW.at[t, :, span(kc)], nssem.at[t, kc], nrsem.at[t, kc], at(prv)).wait_recv()

            depthwise(NEW[t, :, part(kc)], 0, kc, A3)
        for nc in (0, 1):
            first[:, part(nc)] += product(A3, 0, nc)
        for kc in (0, 1):
            depthwise(first[:, part(kc)], 2, kc, B3)
        for nc in (0, 1):
            second[:, part(nc)] = product(B3, 2, nc) + NEW[t, :, part(nc)]
        for kc in (0, 1):
            depthwise(second[:, part(kc)], 3, kc, A3)
        for nc in (0, 1):
            OUT[t, :, part(nc)] = product(A3, 3, nc) + first[:, part(nc)]

            @pl.when((t < TICKS - 1) & (sec < S - 1))
            def _():
                new_copy(t, nc).start()

        @pl.when((t < TICKS - 2) & (sec < S - 2))
        def _():
            ear_copy(t).start()

        out_copy(t).start()
        return carry

    lax.fori_loop(0, TICKS, tick, 0)

    for c in sent:
        c.wait_send()

    @pl.when(sec < S - 1)
    def _():
        old_copy.wait_send()
        for t in range(TICKS - 1):
            for nc in (0, 1):
                new_copy(t, nc).wait_send()

    @pl.when(sec < S - 2)
    def _():
        for t in range(TICKS - 2):
            ear_copy(t).wait_send()

    for t in range(TICKS):
        out_copy(t).wait()


def body(S, Y, pend, stem, spatial, mixing):
    C = mixing.shape[-1]
    T = C // 128
    pend = pend.reshape(2, PIX, C)
    stem = stem.reshape(TICKS - 1, PIX, C)
    flat = jnp.pad(spatial.reshape(36, ROWS), ((0, 28), (0, 0))).reshape(1, 8, 128)
    tiles = mixing.reshape(4, 2, 8, T, 128).transpose(0, 1, 3, 2, 4).reshape(8 * T, 8, 128)
    blk = jnp.concatenate([tiles[:4 * T], flat, tiles[4 * T:]], 0)
    dma = pltpu.SemaphoreType.DMA
    any_ = pl.BlockSpec(memory_space=pl.ANY)
    half = Y // 2
    out = pl.pallas_call(
        functools.partial(kernel, S, Y, C),
        out_shape=jax.ShapeDtypeStruct((TICKS, PIX, C), F32),
        in_specs=[any_] * 3,
        out_specs=any_,
        scratch_shapes=[
            pltpu.VMEM((2, Y, 2, 8 * T + 1, 8, 128), F32),
            pltpu.VMEM((4, 3 * C, C), BF16),
            pltpu.VMEM((PIX, 3 * C), BF16),
            pltpu.VMEM((PIX, 3 * C), BF16),
            pltpu.VMEM((8, 8, C), F32),
            pltpu.VMEM((TICKS, PIX, C), F32),
            pltpu.VMEM((TICKS, PIX, C), F32),
            pltpu.VMEM((TICKS, PIX, C), F32),
            pltpu.VMEM((PIX, C), F32),
            pltpu.VMEM((PIX, C), F32),
            dma((9,)),
            dma((2, 3, half)),
            dma((3, half)),
            dma((3, half)),
            dma((Y + 1,)),
            dma((Y + 1,)),
            dma((4, Y)),
            dma((4, Y)),
            dma((TICKS, 2)),
            dma((TICKS, 2)),
            dma((TICKS,)),
            dma((TICKS,)),
            dma((TICKS,)),
        ],
        compiler_params=pltpu.CompilerParams(collective_id=0, has_side_effects=True, vmem_limit_bytes=60 << 20),
        name="relay",
    )(pend, stem, blk)
    return out.reshape(1, TICKS, 1, GRID, GRID, C)


def solution(mesh):
    S, D = mesh.shape["section"], mesh.shape["dp"]
    placed = (
        P("section", None, "dp", None, None, None),
        P(None, "dp", None, None, None),
        P("section", None, None, "dp"),
        P("section", None, "dp", None),
    )
    return jax.shard_map(
        functools.partial(body, S, D // 4),
        mesh=mesh,
        in_specs=placed,
        out_specs=P("section", None, "dp", None, None, None),
        check_vma=False,
    )
```

```python
import functools

import jax
import jax.numpy as jnp
from jax import lax
from jax.experimental import pallas as pl
from jax.experimental.pallas import tpu as pltpu
from jax.sharding import PartitionSpec as P

MESH = pl.DeviceIdType.MESH
F32, BF16 = jnp.float32, jnp.bfloat16
GRID = 16
PIX = GRID * GRID
TICKS = 4
ROWS = 16
OWN, PAIR, LATE = 0, 1, 2


def kernel(S, Y, C, pend, stem, blk, OUT, G, W3, A3, B3, taps, NEW, EAR, first, second,
           lsem, ssem, fsem, bsem, xssem, xsem, cssem, csem, nssem, nrsem, essem, ersem):
    D = Y * 4
    T = C // 128
    EARLY, ALL = 4 * T + 1, 8 * T + 1
    KC = C // 2
    half = Y // 2
    sec, dp = lax.axis_index("section"), lax.axis_index("dp")
    y, xl, core = dp // 4, lax.rem(dp // 2, 2), lax.rem(dp, 2)
    yup, ydn = lax.rem(dp + 4, D), lax.rem(dp + D - 4, D)
    xpair, cpair = dp + 2 - 4 * xl, dp + 1 - 2 * core
    here = lambda d: {"section": sec, "dp": d}
    at = lambda s: {"section": s, "dp": dp}
    nxt, nxt2 = lax.rem(sec + 1, S), lax.rem(sec + 2, S)
    prv, prv2 = lax.rem(sec + S - 1, S), lax.rem(sec + S - 2, S)

    local = [
        pltpu.make_async_copy(blk, G.at[core, y, xl], lsem.at[0]),
        pltpu.make_async_copy(pend.at[0], EAR.at[0], lsem.at[1]),
        pltpu.make_async_copy(pend.at[1], NEW.at[0], lsem.at[2]),
    ]
    for c in local:
        c.start()
    stems_new = [pltpu.make_async_copy(stem.at[t - 1], NEW.at[t], lsem.at[2 + t]) for t in (1, 2, 3)]
    stems_ear = [pltpu.make_async_copy(stem.at[t - 1], EAR.at[t], lsem.at[5 + t]) for t in (1, 2, 3)]
    stems_one = [pltpu.make_async_copy(stem.at[t - 2], EAR.at[t], lsem.at[5 + t]) for t in (2, 3)]

    @pl.when(sec == 0)
    def _():
        for c in stems_new + stems_ear:
            c.start()

    @pl.when(sec == 1)
    def _():
        for c in stems_one:
            c.start()

    barrier = pltpu.get_barrier_semaphore()
    for d in (here(yup), here(ydn), here(xpair), here(cpair), at(nxt), at(prv), at(nxt2), at(prv2)):
        pl.semaphore_signal(barrier, inc=1, device_id=d, device_id_type=MESH)
    pl.semaphore_wait(barrier, 8)
    local[0].wait()

    sent = []

    def remote(src, dst, s, r, dev):
        return pltpu.make_async_remote_copy(src_ref=src, dst_ref=dst, send_sem=s, recv_sem=r,
                                            device_id=dev, device_id_type=MESH)

    def send(c):
        c.start()
        sent.append(c)

    def piece(cc, yy, xx, late):
        lo, n = (EARLY, ALL - EARLY) if late else (0, EARLY)
        return G.at[cc, yy, xx, pl.ds(lo, n)]

    def ring(way, stream, k):
        yy = lax.rem(y + Y - (k - 1), Y) if way == 0 else lax.rem(y + (k - 1), Y)
        xx = 1 - xl if stream == PAIR else xl
        p = piece(core, yy, xx, stream == LATE)
        sems = fsem if way == 0 else bsem
        return remote(p, p, ssem.at[way, stream, k - 1], sems.at[stream, k - 1], here(yup if way == 0 else ydn))

    def carried(way, stream, k):
        if k < half:
            return True
        return k == half and (way == 1 if stream == PAIR else way == 0)

    def arrived(way, stream, k):
        yy = lax.rem(y + Y - k, Y) if way == 0 else lax.rem(y + k, Y)
        xx = 1 - xl if stream == PAIR else xl
        p = piece(core, yy, xx, stream == LATE)
        sems = fsem if way == 0 else bsem
        remote(p, p, ssem.at[way, stream, k - 1], sems.at[stream, k - 1], here(ydn)).wait_recv()
        return yy, xx

    def slot(way, k):
        return 0 if k == 0 else (k if way == 0 else Y - k)

    def cross(way, k):
        yy = lax.rem(y + Y - k, Y) if way == 0 else lax.rem(y + k, Y)
        p = piece(core, yy, xl, True)
        n = slot(way, k)
        return remote(p, p, xssem.at[n], xsem.at[n], here(xpair))

    def crossed(way, k):
        yy = lax.rem(y + Y - k, Y) if way == 0 else lax.rem(y + k, Y)
        p = piece(core, yy, 1 - xl, True)
        n = slot(way, k)
        remote(p, p, xssem.at[n], xsem.at[n], here(xpair)).wait_recv()
        return yy, 1 - xl

    def share(yy, xx, late, way, k, pair):
        n = (2 if pair else 0) + (1 if late else 0)
        p = piece(core, yy, xx, late)
        send(remote(p, p, cssem.at[n, slot(way, k)], csem.at[n, slot(way, k)], here(cpair)))

    def shared(yy, xx, late, way, k, pair):
        n = (2 if pair else 0) + (1 if late else 0)
        p = piece(1 - core, yy, xx, late)
        remote(p, p, cssem.at[n, slot(way, k)], csem.at[n, slot(way, k)], here(cpair)).wait_recv()

    def split(cc, yy, xx, late):
        row = pl.multiple_of(((yy * 2 + xx) * 2 + cc) * ROWS, ROWS)
        base = EARLY if late else 0

        def step(m, carry):
            b = (2 if late else 0) + m
            for j in range(T):
                w = jnp.concatenate([G[cc, yy, xx, base + m * 2 * T + j], G[cc, yy, xx, base + m * 2 * T + T + j]], 0)
                hi = w.astype(BF16)
                lo = (w - hi.astype(F32)).astype(BF16)
                lanes = slice(128 * j, 128 * j + 128)
                W3[b, pl.ds(row, ROWS), lanes] = hi
                W3[b, pl.ds(pl.multiple_of(C + row, ROWS), ROWS), lanes] = hi
                W3[b, pl.ds(pl.multiple_of(2 * C + row, ROWS), ROWS), lanes] = lo
            return carry

        lax.fori_loop(0, 2, step, 0)

    own = piece(core, y, xl, False)
    send(remote(own, own, xssem.at[Y], xsem.at[Y], here(xpair)))
    for stream in (OWN, LATE):
        for way in (0, 1):
            if carried(way, stream, 1):
                send(ring(way, stream, 1))
    send(cross(0, 0))
    share(y, xl, False, 0, 0, False)
    share(y, xl, True, 0, 0, False)

    old_copy = remote(pend.at[1], EAR.at[1], essem.at[1], ersem.at[1], at(nxt))

    @pl.when(sec < S - 1)
    def _():
        old_copy.start()

    split(core, y, xl, False)
    split(core, y, xl, True)
    other = piece(core, y, 1 - xl, False)
    remote(other, other, xssem.at[Y], xsem.at[Y], here(xpair)).wait_recv()
    for way in (0, 1):
        if carried(way, PAIR, 1):
            send(ring(way, PAIR, 1))
    share(y, 1 - xl, False, 0, 0, True)
    split(core, y, 1 - xl, False)

    def tail(ways, k):
        for way in ways:
            yy, xx = crossed(way, k)
            share(yy, xx, True, way, k, True)
            split(core, yy, xx, True)
        for way in ways:
            yy = lax.rem(y + Y - k, Y) if way == 0 else lax.rem(y + k, Y)
            for pair in (False, True):
                xx = 1 - xl if pair else xl
                for late in (False, True):
                    shared(yy, xx, late, way, k, pair)
                    split(1 - core, yy, xx, late)

    for k in range(1, half + 1):
        got = []
        for stream in (LATE, OWN, PAIR):
            for way in (0, 1):
                if not carried(way, stream, k):
                    continue
                yy, xx = arrived(way, stream, k)
                if carried(way, stream, k + 1):
                    send(ring(way, stream, k + 1))
                late = stream == LATE
                w = 0 if k == half else way
                if late:
                    send(cross(w, k))
                share(yy, xx, late, w, k, stream == PAIR)
                got.append((yy, xx, late))
        for yy, xx, late in got:
            split(core, yy, xx, late)
        tail((0,) if k == 1 else (0, 1), k - 1)
    tail((0,), half)

    lane = lax.broadcasted_iota(jnp.int32, (8, 128), 1) // ROWS

    def gather_taps(g, carry):
        lanes = pl.ds(pl.multiple_of(g * 128, 128), 128)
        tiles = [G[e % 2, 2 * g + e // 4, (e // 2) % 2, EARLY - 1] for e in range(8)]
        for q in range(8):
            row = jnp.zeros((8, 128), F32)
            for e in range(8):
                shift = ((e - q) % 8) * ROWS
                moved = pltpu.roll(tiles[e], shift, 1) if shift else tiles[e]
                row = jnp.where(lane == e, moved, row)
            taps[q, :, lanes] = row
        return carry

    lax.fori_loop(0, T, gather_taps, 0)

    for c in local[1:]:
        c.wait()

    @pl.when(sec == 0)
    def _():
        for c in stems_new + stems_ear:
            c.wait()

    @pl.when(sec == 1)
    def _():
        for c in stems_one:
            c.wait()

    def tap(b, t, kc):
        n = 9 * b + t
        return taps[n % 8, n // 8:n // 8 + 1, kc * KC:(kc + 1) * KC].reshape(1, 1, KC)

    col = lax.broadcasted_iota(jnp.int32, (1, GRID, KC), 1)

    def depthwise(v, b, kc, acts):
        v = jnp.maximum(v.reshape(GRID, GRID, KC), 0.0)
        left, right = pltpu.roll(v, 1, 1), pltpu.roll(v, GRID - 1, 1)
        rows = []
        for i in range(3):
            kl = jnp.where(col == 0, 0.0, jnp.broadcast_to(tap(b, 3 * i, kc), (1, GRID, KC)))
            kr = jnp.where(col == GRID - 1, 0.0, jnp.broadcast_to(tap(b, 3 * i + 2, kc), (1, GRID, KC)))
            rows.append(left * kl + v * tap(b, 3 * i + 1, kc) + right * kr)
        zero = jnp.zeros((1, GRID, KC), F32)
        total = (jnp.concatenate([zero, rows[0][:GRID - 1]], 0) + rows[1]
                 + jnp.concatenate([rows[2][1:], zero], 0)).reshape(PIX, KC)
        hi = total.astype(BF16)
        lo = (total - hi.astype(F32)).astype(BF16)
        acts[:, kc * KC:(kc + 1) * KC] = hi
        acts[:, C + kc * KC:C + (kc + 1) * KC] = lo
        acts[:, 2 * C + kc * KC:2 * C + (kc + 1) * KC] = hi

    def product(acts, b, nc):
        return jnp.dot(acts[...], W3[b, :, nc * KC:(nc + 1) * KC], preferred_element_type=F32)

    part = lambda nc: slice(nc * KC, (nc + 1) * KC)
    span = lambda nc: pl.ds(nc * KC, KC)

    def new_copy(t, nc):
        return remote(OUT.at[t, :, span(nc)], NEW.at[t + 1, :, span(nc)], nssem.at[t, nc], nrsem.at[t + 1, nc], at(nxt))

    def ear_copy(t):
        return remote(OUT.at[t], EAR.at[t + 2], essem.at[t + 2], ersem.at[t + 2], at(nxt2))

    def tick(t, carry):
        @pl.when(((t == 1) & (sec > 0)) | ((t > 1) & (sec > 1)))
        def _():
            remote(EAR.at[t], EAR.at[t], essem.at[t], ersem.at[t], at(prv)).wait_recv()

        for kc in (0, 1):
            depthwise(EAR[t, :, part(kc)], 1, kc, B3)
        for nc in (0, 1):
            first[:, part(nc)] = product(B3, 1, nc)
        for kc in (0, 1):
            @pl.when((t > 0) & (sec > 0))
            def _():
                remote(NEW.at[t, :, span(kc)], NEW.at[t, :, span(kc)], nssem.at[t, kc], nrsem.at[t, kc], at(prv)).wait_recv()

            depthwise(NEW[t, :, part(kc)], 0, kc, A3)
        for nc in (0, 1):
            first[:, part(nc)] += product(A3, 0, nc)
        for kc in (0, 1):
            depthwise(first[:, part(kc)], 2, kc, B3)
        for nc in (0, 1):
            second[:, part(nc)] = product(B3, 2, nc) + NEW[t, :, part(nc)]
        for kc in (0, 1):
            depthwise(second[:, part(kc)], 3, kc, A3)
        for nc in (0, 1):
            OUT[t, :, part(nc)] = product(A3, 3, nc) + first[:, part(nc)]

            @pl.when((t < TICKS - 1) & (sec < S - 1))
            def _():
                new_copy(t, nc).start()

        @pl.when((t < TICKS - 2) & (sec < S - 2))
        def _():
            ear_copy(t).start()

        return carry

    lax.fori_loop(0, TICKS, tick, 0)

    for c in sent:
        c.wait_send()

    @pl.when(sec < S - 1)
    def _():
        old_copy.wait_send()
        for t in range(TICKS - 1):
            for nc in (0, 1):
                new_copy(t, nc).wait_send()

    @pl.when(sec < S - 2)
    def _():
        for t in range(TICKS - 2):
            ear_copy(t).wait_send()


def body(S, Y, pend, stem, spatial, mixing):
    C = mixing.shape[-1]
    T = C // 128
    pend = pend.reshape(2, PIX, C)
    stem = stem.reshape(TICKS - 1, PIX, C)
    flat = jnp.pad(spatial.reshape(36, ROWS), ((0, 28), (0, 0))).reshape(1, 8, 128)
    tiles = mixing.reshape(4, 2, 8, T, 128).transpose(0, 1, 3, 2, 4).reshape(8 * T, 8, 128)
    blk = jnp.concatenate([tiles[:4 * T], flat, tiles[4 * T:]], 0)
    dma = pltpu.SemaphoreType.DMA
    any_ = pl.BlockSpec(memory_space=pl.ANY)
    half = Y // 2
    out = pl.pallas_call(
        functools.partial(kernel, S, Y, C),
        out_shape=jax.ShapeDtypeStruct((TICKS, PIX, C), F32),
        in_specs=[any_] * 3,
        out_specs=pl.BlockSpec(memory_space=pltpu.VMEM),
        scratch_shapes=[
            pltpu.VMEM((2, Y, 2, 8 * T + 1, 8, 128), F32),
            pltpu.VMEM((4, 3 * C, C), BF16),
            pltpu.VMEM((PIX, 3 * C), BF16),
            pltpu.VMEM((PIX, 3 * C), BF16),
            pltpu.VMEM((8, 8, C), F32),
            pltpu.VMEM((TICKS, PIX, C), F32),
            pltpu.VMEM((TICKS, PIX, C), F32),
            pltpu.VMEM((PIX, C), F32),
            pltpu.VMEM((PIX, C), F32),
            dma((9,)),
            dma((2, 3, half)),
            dma((3, half)),
            dma((3, half)),
            dma((Y + 1,)),
            dma((Y + 1,)),
            dma((4, Y)),
            dma((4, Y)),
            dma((TICKS, 2)),
            dma((TICKS, 2)),
            dma((TICKS,)),
            dma((TICKS,)),
        ],
        compiler_params=pltpu.CompilerParams(collective_id=0, has_side_effects=True, vmem_limit_bytes=24 << 20),
        name="relay",
    )(pend, stem, blk)
    return out.reshape(1, TICKS, 1, GRID, GRID, C)


def solution(mesh):
    S, D = mesh.shape["section"], mesh.shape["dp"]
    placed = (
        P("section", None, "dp", None, None, None),
        P(None, "dp", None, None, None),
        P("section", None, None, "dp"),
        P("section", None, "dp", None),
    )
    return jax.shard_map(
        functools.partial(body, S, D // 4),
        mesh=mesh,
        in_specs=placed,
        out_specs=P("section", None, "dp", None, None, None),
        check_vma=False,
    )
```

```python
import functools

import jax
import jax.numpy as jnp
from jax import lax
from jax.experimental import pallas as pl
from jax.experimental.pallas import tpu as pltpu
from jax.sharding import PartitionSpec as P

MESH = pl.DeviceIdType.MESH
F32, BF16 = jnp.float32, jnp.bfloat16
GRID = 16
PIX = GRID * GRID
TICKS = 4
ROWS = 16
OWN, PAIR, LATE, TWIN, TWIN_PAIR = range(5)


def kernel(S, Y, C, pend, stem, blk, OUT, G, W3, A3, B3, taps, BUF, first, second,
           lsem, ssem, rsem, xssem, xsem, ossem, orsem, cssem, csem, mssem, mrsem):
    D = Y * 4
    T = C // 128
    EARLY, ALL = 4 * T + 1, 8 * T + 1
    KC = C // 2
    half = Y // 2
    sec, dp = lax.axis_index("section"), lax.axis_index("dp")
    odd = lax.rem(sec, 2)
    y, xl, core = dp // 4, lax.rem(dp // 2, 2), lax.rem(dp, 2)
    yup, ydn = lax.rem(dp + 4, D), lax.rem(dp + D - 4, D)
    xpair, cpair = dp + 2 - 4 * xl, dp + 1 - 2 * core
    twin = sec + 1 - 2 * odd
    here = lambda d: {"section": sec, "dp": d}
    at = lambda s: {"section": s, "dp": dp}
    there = lambda d: {"section": twin, "dp": d}
    nxt, nxt2 = lax.rem(sec + 1, S), lax.rem(sec + 2, S)
    prv, prv2 = lax.rem(sec + S - 1, S), lax.rem(sec + S - 2, S)

    local = [
        pltpu.make_async_copy(blk, G.at[0, core, y, xl], lsem.at[0]),
        pltpu.make_async_copy(pend.at[0], BUF.at[0], lsem.at[1]),
        pltpu.make_async_copy(pend.at[1], BUF.at[1], lsem.at[2]),
    ]
    for c in local:
        c.start()
    stems_zero = [pltpu.make_async_copy(stem.at[n], BUF.at[m], lsem.at[m]) for n, m in ((1, 4), (1, 5), (2, 6), (2, 7))]
    stems_one = [pltpu.make_async_copy(stem.at[n], BUF.at[m], lsem.at[m + 6]) for n, m in ((0, 2), (0, 3), (1, 6))]

    @pl.when(sec == 0)
    def _():
        for c in stems_zero:
            c.start()

    @pl.when(sec == 1)
    def _():
        for c in stems_one:
            c.start()

    barrier = pltpu.get_barrier_semaphore()
    partners = (here(yup), here(ydn), here(xpair), here(cpair), there(dp), there(xpair), at(nxt), at(prv), at(nxt2), at(prv2))
    for d in partners:
        pl.semaphore_signal(barrier, inc=1, device_id=d, device_id_type=MESH)
    pl.semaphore_wait(barrier, len(partners))
    local[0].wait()

    sent = []

    def remote(src, dst, s, r, dev):
        return pltpu.make_async_remote_copy(src_ref=src, dst_ref=dst, send_sem=s, recv_sem=r,
                                            device_id=dev, device_id_type=MESH)

    def send(c):
        c.start()
        sent.append(c)

    def piece(p, cc, yy, xx, late):
        lo, n = (EARLY, ALL - EARLY) if late else (0, EARLY)
        return G.at[p, cc, yy, xx, pl.ds(lo, n)]

    def column(stream):
        return xl if stream in (OWN, LATE, TWIN) else 1 - xl

    def place(way, k):
        return lax.rem(y + Y - k, Y) if way == 0 else lax.rem(y + k, Y)

    def ring_piece(stream, yy):
        return piece(1 if stream >= TWIN else 0, core, yy, column(stream), stream == LATE)

    def ring(way, stream, k):
        p = ring_piece(stream, place(way, k - 1))
        return remote(p, p, ssem.at[way, stream, k - 1], rsem.at[way, stream, k - 1], here(yup if way == 0 else ydn))

    def carried(way, stream, k):
        return k < half or (k == half and way == (1 if stream in (PAIR, TWIN_PAIR) else 0))

    def arrived(way, stream, k):
        yy = place(way, k)
        p = ring_piece(stream, yy)
        remote(p, p, ssem.at[way, stream, k - 1], rsem.at[way, stream, k - 1], here(ydn)).wait_recv()
        return yy

    def slot(way, k):
        return 0 if k == 0 else (k if way == 0 else Y - k)

    def cross(way, k):
        p = piece(0, core, place(way, k), xl, True)
        return remote(p, p, xssem.at[slot(way, k)], xsem.at[slot(way, k)], here(xpair))

    def crossed(way, k):
        p = piece(0, core, place(way, k), 1 - xl, True)
        remote(p, p, xssem.at[slot(way, k)], xsem.at[slot(way, k)], here(xpair)).wait_recv()

    def over(far, yy, late, n):
        return remote(piece(0, core, yy, xl, late), piece(1, core, yy, xl, late), ossem.at[far, n], orsem.at[far, n],
                      there(xpair if far else dp))

    def came_over(far, yy, late, n):
        p = piece(1, core, yy, 1 - xl if far else xl, late)
        remote(p, p, ossem.at[far, n], orsem.at[far, n], there(dp)).wait_recv()

    def share(p, yy, other, late, n):
        q, m = piece(p, core, yy, 1 - xl if other else xl, late), 4 * p + 2 * other + late
        send(remote(q, q, cssem.at[m, n], csem.at[m, n], here(cpair)))

    def shared(p, yy, other, late, n):
        q, m = piece(p, 1 - core, yy, 1 - xl if other else xl, late), 4 * p + 2 * other + late
        remote(q, q, cssem.at[m, n], csem.at[m, n], here(cpair)).wait_recv()

    def split(p, cc, yy, xx, late):
        row = pl.multiple_of(((yy * 2 + xx) * 2 + cc) * ROWS, ROWS)
        base = EARLY if late else 0

        def step(m, carry):
            b = 4 * p + (2 if late else 0) + m
            for j in range(T):
                w = jnp.concatenate([G[p, cc, yy, xx, base + m * 2 * T + j], G[p, cc, yy, xx, base + m * 2 * T + T + j]], 0)
                hi = w.astype(BF16)
                lo = (w - hi.astype(F32)).astype(BF16)
                lanes = slice(128 * j, 128 * j + 128)
                W3[b, pl.ds(row, ROWS), lanes] = hi
                W3[b, pl.ds(pl.multiple_of(C + row, ROWS), ROWS), lanes] = hi
                W3[b, pl.ds(pl.multiple_of(2 * C + row, ROWS), ROWS), lanes] = lo
            return carry

        lax.fori_loop(0, 2, step, 0)

    def both(k):
        return (0,) if k in (0, half) else (0, 1)

    def from_core(p, k):
        for way in both(k):
            yy = place(way, k)
            for other in (0, 1):
                for late in (0, 1):
                    shared(p, yy, other, late, slot(way, k))
                    split(p, 1 - core, yy, 1 - xl if other else xl, late)

    def ring_step(streams, k):
        got = []
        for stream in streams:
            for way in (0, 1):
                if not carried(way, stream, k):
                    continue
                yy = arrived(way, stream, k)
                if carried(way, stream, k + 1):
                    send(ring(way, stream, k + 1))
                n = slot(way, k)
                if stream == LATE:
                    send(cross(way, k))
                p = 1 if stream >= TWIN else 0
                share(p, yy, 1 if stream in (PAIR, TWIN_PAIR) else 0, 1 if stream == LATE else 0, n)
                got.append((p, yy, column(stream), stream == LATE))
        for p, yy, xx, late in got:
            split(p, core, yy, xx, late)

    def own_tail(k):
        for way in both(k):
            crossed(way, k)
            share(0, place(way, k), 1, 1, slot(way, k))
            split(0, core, place(way, k), 1 - xl, True)
        from_core(0, k)

    def send_over(k):
        for way in both(k):
            for far in (0, 1):
                send(over(far, place(way, k), True, slot(way, k)))

    def twin_tail(k):
        for way in both(k):
            for far in (0, 1):
                yy = place(way, k)
                came_over(far, yy, True, slot(way, k))
                share(1, yy, far, 1, slot(way, k))
                split(1, core, yy, 1 - xl if far else xl, True)

    own = piece(0, core, y, xl, False)
    send(remote(own, own, xssem.at[Y], xsem.at[Y], here(xpair)))
    for stream in (OWN, LATE):
        for way in (0, 1):
            if carried(way, stream, 1):
                send(ring(way, stream, 1))
    send(cross(0, 0))
    share(0, y, 0, 0, 0)
    share(0, y, 0, 1, 0)
    for far in (0, 1):
        send(over(far, y, False, Y))
    old_copy = remote(pend.at[1], BUF.at[2], mssem.at[2, 0], mrsem.at[2, 0], at(nxt2))

    @pl.when((odd == 1) & (sec < S - 2))
    def _():
        old_copy.start()

    split(0, core, y, xl, False)
    split(0, core, y, xl, True)
    other_own = piece(0, core, y, 1 - xl, False)
    remote(other_own, other_own, xssem.at[Y], xsem.at[Y], here(xpair)).wait_recv()
    for way in (0, 1):
        if carried(way, PAIR, 1):
            send(ring(way, PAIR, 1))
    share(0, y, 1, 0, 0)
    split(0, core, y, 1 - xl, False)

    def start_twin():
        for far in (0, 1):
            came_over(far, y, False, Y)
            for way in (0, 1):
                stream = TWIN_PAIR if far else TWIN
                if carried(way, stream, 1):
                    send(ring(way, stream, 1))
            share(1, y, far, 0, 0)
            split(1, core, y, 1 - xl if far else xl, False)

    LAG = 2
    for k in range(1, half + 1):
        ring_step((LATE, OWN, PAIR), k)
        own_tail(k - 1)
        send_over(k - 1)
        if k == min(LAG, half):
            start_twin()
        if k > LAG:
            ring_step((TWIN, TWIN_PAIR), k - LAG)
    own_tail(half)
    send_over(half)

    lane = lax.broadcasted_iota(jnp.int32, (8, 128), 1) // ROWS

    def gather_taps(p):
        def step(g, carry):
            lanes = pl.ds(pl.multiple_of(g * 128, 128), 128)
            tiles = [G[p, e % 2, 2 * g + e // 4, (e // 2) % 2, EARLY - 1] for e in range(8)]
            for q in range(8):
                row = jnp.zeros((8, 128), F32)
                for e in range(8):
                    shift = ((e - q) % 8) * ROWS
                    moved = pltpu.roll(tiles[e], shift, 1) if shift else tiles[e]
                    row = jnp.where(lane == e, moved, row)
                taps[p, q, :, lanes] = row
            return carry

        lax.fori_loop(0, T, step, 0)

    gather_taps(0)
    for c in local[1:]:
        c.wait()

    @pl.when(sec == 0)
    def _():
        for c in stems_zero:
            c.wait()

    @pl.when(sec == 1)
    def _():
        for c in stems_one:
            c.wait()

    col = lax.broadcasted_iota(jnp.int32, (1, GRID, KC), 1)

    def depthwise(v, p, b, kc, acts):
        def tap(t):
            n = 9 * b + t
            return taps[p, n % 8, n // 8:n // 8 + 1, kc * KC:(kc + 1) * KC].reshape(1, 1, KC)

        v = jnp.maximum(v.reshape(GRID, GRID, KC), 0.0)
        left, right = pltpu.roll(v, 1, 1), pltpu.roll(v, GRID - 1, 1)
        rows = []
        for i in range(3):
            kl = jnp.where(col == 0, 0.0, jnp.broadcast_to(tap(3 * i), (1, GRID, KC)))
            kr = jnp.where(col == GRID - 1, 0.0, jnp.broadcast_to(tap(3 * i + 2), (1, GRID, KC)))
            rows.append(left * kl + v * tap(3 * i + 1) + right * kr)
        zero = jnp.zeros((1, GRID, KC), F32)
        total = (jnp.concatenate([zero, rows[0][:GRID - 1]], 0) + rows[1]
                 + jnp.concatenate([rows[2][1:], zero], 0)).reshape(PIX, KC)
        hi = total.astype(BF16)
        lo = (total - hi.astype(F32)).astype(BF16)
        acts[:, kc * KC:(kc + 1) * KC] = hi
        acts[:, C + kc * KC:C + (kc + 1) * KC] = lo
        acts[:, 2 * C + kc * KC:2 * C + (kc + 1) * KC] = hi

    part = lambda nc: slice(nc * KC, (nc + 1) * KC)
    span = lambda nc: pl.ds(nc * KC, KC)

    def landed(m, nc):
        r = BUF.at[m, :, span(nc)]
        remote(r, r, mssem.at[m, nc], mrsem.at[m, nc], at(prv)).wait_recv()

    def pass_on(t, m, nc, dev):
        return remote(BUF.at[8 + t, :, span(nc)], BUF.at[m, :, span(nc)], mssem.at[m, nc], mrsem.at[m, nc], dev)

    up0 = lambda nc: pass_on(0, 4 - odd, nc, at(nxt2))
    up1 = lambda nc: pass_on(1, 5, nc, at(nxt2))
    up2 = lambda nc: pass_on(2, 7, nc, at(nxt))
    home = remote(BUF.at[9], OUT.at[1], mssem.at[8, 0], mrsem.at[8, 0], there(dp))
    again = remote(OUT.at[1], BUF.at[6], mssem.at[6, 0], mrsem.at[6, 0], at(nxt2))

    def cell(t, p):
        ear = jnp.where(t == 0, 0, jnp.where(t == 1, 1 + odd, jnp.where(t == 2, 4 - odd, 6)))
        new = jnp.where(t == 0, 1, jnp.where(t == 1, 8 - 5 * odd, jnp.where(t == 2, 5 + 4 * odd, 7)))

        def product(acts, b, nc):
            return jnp.dot(acts[...], W3[4 * p + b, :, nc * KC:(nc + 1) * KC], preferred_element_type=F32)

        @pl.when((t == 1) & (odd == 1) & (sec > 1))
        def _():
            r = BUF.at[2]
            remote(r, r, mssem.at[2, 0], mrsem.at[2, 0], at(prv2)).wait_recv()

        @pl.when((t == 2) & (odd == 0) & (sec > 1))
        def _():
            landed(4, 0)
            landed(4, 1)

        @pl.when((t == 3) & (sec > 1))
        def _():
            r = BUF.at[6]
            remote(r, r, mssem.at[6, 0], mrsem.at[6, 0], at(prv2)).wait_recv()

        for kc in (0, 1):
            depthwise(BUF[ear, :, part(kc)], p, 1, kc, B3)
        for nc in (0, 1):
            first[:, part(nc)] = product(B3, 1, nc)
        for kc in (0, 1):
            @pl.when((t == 1) & (odd == 1) & (sec > 1))
            def _():
                landed(3, kc)

            @pl.when((t == 2) & (odd == 0) & (sec > 1))
            def _():
                landed(5, kc)

            @pl.when((t == 3) & (sec > 0))
            def _():
                landed(7, kc)

            depthwise(BUF[new, :, part(kc)], p, 0, kc, A3)
        for nc in (0, 1):
            first[:, part(nc)] += product(A3, 0, nc)
        for kc in (0, 1):
            depthwise(first[:, part(kc)], p, 2, kc, B3)
        for nc in (0, 1):
            second[:, part(nc)] = product(B3, 2, nc) + BUF[new, :, part(nc)]
        for kc in (0, 1):
            depthwise(second[:, part(kc)], p, 3, kc, A3)
        for nc in (0, 1):
            v = product(A3, 3, nc) + first[:, part(nc)]
            BUF[8 + t, :, part(nc)] = v

            @pl.when(t != 1)
            def _():
                OUT[t, :, part(nc)] = v

            @pl.when((t == 0) & (sec < S - 2))
            def _():
                up0(nc).start()

            @pl.when((t == 1) & (odd == 0) & (sec < S - 2))
            def _():
                up1(nc).start()

            @pl.when((t == 2) & (sec < S - 1))
            def _():
                up2(nc).start()

        @pl.when(t == 1)
        def _():
            home.start()

        @pl.when(t == 2)
        def _():
            home.wait_recv()

        @pl.when((t == 2) & (sec < S - 2))
        def _():
            again.start()

    cell(jnp.int32(0), 0)

    for k in range(max(half - LAG, 0) + 1, half + 1):
        ring_step((TWIN, TWIN_PAIR), k)
    for k in range(half + 1):
        twin_tail(k)
    for k in range(half + 1):
        from_core(1, k)
    gather_taps(1)

    def tick(t, carry):
        cell(t, jnp.where(t == 1, 1, 0))
        return carry

    lax.fori_loop(1, TICKS, tick, 0)

    for c in sent:
        c.wait_send()
    home.wait_send()

    @pl.when((odd == 1) & (sec < S - 2))
    def _():
        old_copy.wait_send()

    @pl.when(sec < S - 2)
    def _():
        for nc in (0, 1):
            up0(nc).wait_send()
        again.wait_send()

    @pl.when((odd == 0) & (sec < S - 2))
    def _():
        for nc in (0, 1):
            up1(nc).wait_send()

    @pl.when(sec < S - 1)
    def _():
        for nc in (0, 1):
            up2(nc).wait_send()


def body(S, Y, pend, stem, spatial, mixing):
    C = mixing.shape[-1]
    T = C // 128
    pend = pend.reshape(2, PIX, C)
    stem = stem.reshape(TICKS - 1, PIX, C)
    flat = jnp.pad(spatial.reshape(36, ROWS), ((0, 28), (0, 0))).reshape(1, 8, 128)
    tiles = mixing.reshape(4, 2, 8, T, 128).transpose(0, 1, 3, 2, 4).reshape(8 * T, 8, 128)
    blk = jnp.concatenate([tiles[:4 * T], flat, tiles[4 * T:]], 0)
    dma = pltpu.SemaphoreType.DMA
    any_ = pl.BlockSpec(memory_space=pl.ANY)
    half = Y // 2
    out = pl.pallas_call(
        functools.partial(kernel, S, Y, C),
        out_shape=jax.ShapeDtypeStruct((TICKS, PIX, C), F32),
        in_specs=[any_] * 3,
        out_specs=pl.BlockSpec(memory_space=pltpu.VMEM),
        scratch_shapes=[
            pltpu.VMEM((2, 2, Y, 2, 8 * T + 1, 8, 128), F32),
            pltpu.VMEM((8, 3 * C, C), BF16),
            pltpu.VMEM((PIX, 3 * C), BF16),
            pltpu.VMEM((PIX, 3 * C), BF16),
            pltpu.VMEM((2, 8, 8, C), F32),
            pltpu.VMEM((12, PIX, C), F32),
            pltpu.VMEM((PIX, C), F32),
            pltpu.VMEM((PIX, C), F32),
            dma((13,)),
            dma((2, 5, half)),
            dma((2, 5, half)),
            dma((Y + 1,)),
            dma((Y + 1,)),
            dma((2, Y + 1)),
            dma((2, Y + 1)),
            dma((8, Y)),
            dma((8, Y)),
            dma((9, 2)),
            dma((9, 2)),
        ],
        compiler_params=pltpu.CompilerParams(collective_id=0, has_side_effects=True, vmem_limit_bytes=38 << 20),
        name="relay",
    )(pend, stem, blk)
    return out.reshape(1, TICKS, 1, GRID, GRID, C)


def solution(mesh):
    S, D = mesh.shape["section"], mesh.shape["dp"]
    placed = (
        P("section", None, "dp", None, None, None),
        P(None, "dp", None, None, None),
        P("section", None, None, "dp"),
        P("section", None, "dp", None),
    )
    return jax.shard_map(
        functools.partial(body, S, D // 4),
        mesh=mesh,
        in_specs=placed,
        out_specs=P("section", None, "dp", None, None, None),
        check_vma=False,
    )
```

```python
import functools

import jax
import jax.numpy as jnp
from jax import lax
from jax.experimental import pallas as pl
from jax.experimental.pallas import tpu as pltpu
from jax.sharding import PartitionSpec as P

MESH = pl.DeviceIdType.MESH
F32, BF16 = jnp.float32, jnp.bfloat16
GRID = 16
PIX = GRID * GRID
TICKS = 4
ROWS = 16
OWN, PAIR, LATE, TWIN, TWIN_PAIR = range(5)


def kernel(S, Y, C, pend, stem, blk, OUT, G, W3, A3, B3, taps, BUF, first, second,
           lsem, ssem, rsem, xssem, xsem, ossem, orsem, cssem, csem, mssem, mrsem):
    D = Y * 4
    T = C // 128
    EARLY, ALL = 4 * T + 1, 8 * T + 1
    KC = C // 2
    half = Y // 2
    sec, dp = lax.axis_index("section"), lax.axis_index("dp")
    odd = lax.rem(sec, 2)
    y, xl, core = dp // 4, lax.rem(dp // 2, 2), lax.rem(dp, 2)
    yup, ydn = lax.rem(dp + 4, D), lax.rem(dp + D - 4, D)
    xpair, cpair = dp + 2 - 4 * xl, dp + 1 - 2 * core
    twin = sec + 1 - 2 * odd
    here = lambda d: {"section": sec, "dp": d}
    at = lambda s: {"section": s, "dp": dp}
    there = lambda d: {"section": twin, "dp": d}
    nxt, nxt2 = lax.rem(sec + 1, S), lax.rem(sec + 2, S)
    prv, prv2 = lax.rem(sec + S - 1, S), lax.rem(sec + S - 2, S)

    local = [
        pltpu.make_async_copy(blk, G.at[0, core, y, xl], lsem.at[0]),
        pltpu.make_async_copy(pend.at[0], BUF.at[0], lsem.at[1]),
        pltpu.make_async_copy(pend.at[1], BUF.at[1], lsem.at[2]),
    ]
    for c in local:
        c.start()
    stems_zero = [pltpu.make_async_copy(stem.at[n], BUF.at[m], lsem.at[m]) for n, m in ((1, 4), (1, 5), (2, 6), (2, 7))]
    stems_one = [pltpu.make_async_copy(stem.at[n], BUF.at[m], lsem.at[m + 6]) for n, m in ((0, 2), (0, 3), (1, 6))]

    @pl.when(sec == 0)
    def _():
        for c in stems_zero:
            c.start()

    @pl.when(sec == 1)
    def _():
        for c in stems_one:
            c.start()

    barrier = pltpu.get_barrier_semaphore()
    partners = (here(yup), here(ydn), here(xpair), here(cpair), there(dp), there(xpair), at(nxt), at(prv), at(nxt2), at(prv2))
    for d in partners:
        pl.semaphore_signal(barrier, inc=1, device_id=d, device_id_type=MESH)
    pl.semaphore_wait(barrier, len(partners))
    local[0].wait()

    sent = []

    def remote(src, dst, s, r, dev):
        return pltpu.make_async_remote_copy(src_ref=src, dst_ref=dst, send_sem=s, recv_sem=r,
                                            device_id=dev, device_id_type=MESH)

    def send(c):
        c.start()
        sent.append(c)

    def piece(p, cc, yy, xx, late):
        lo, n = (EARLY, ALL - EARLY) if late else (0, EARLY)
        return G.at[p, cc, yy, xx, pl.ds(lo, n)]

    def column(stream):
        return xl if stream in (OWN, LATE, TWIN) else 1 - xl

    def place(way, k):
        return lax.rem(y + Y - k, Y) if way == 0 else lax.rem(y + k, Y)

    def ring_piece(stream, yy):
        return piece(1 if stream >= TWIN else 0, core, yy, column(stream), stream == LATE)

    def ring(way, stream, k):
        p = ring_piece(stream, place(way, k - 1))
        return remote(p, p, ssem.at[way, stream, k - 1], rsem.at[way, stream, k - 1], here(yup if way == 0 else ydn))

    def carried(way, stream, k):
        return k < half or (k == half and way == (1 if stream in (PAIR, TWIN_PAIR) else 0))

    def arrived(way, stream, k):
        yy = place(way, k)
        p = ring_piece(stream, yy)
        remote(p, p, ssem.at[way, stream, k - 1], rsem.at[way, stream, k - 1], here(ydn)).wait_recv()
        return yy

    def slot(way, k):
        return 0 if k == 0 else (k if way == 0 else Y - k)

    def cross(way, k):
        p = piece(0, core, place(way, k), xl, True)
        return remote(p, p, xssem.at[slot(way, k)], xsem.at[slot(way, k)], here(xpair))

    def crossed(way, k):
        p = piece(0, core, place(way, k), 1 - xl, True)
        remote(p, p, xssem.at[slot(way, k)], xsem.at[slot(way, k)], here(xpair)).wait_recv()

    def over(far, yy, late, n):
        return remote(piece(0, core, yy, xl, late), piece(1, core, yy, xl, late), ossem.at[far, n], orsem.at[far, n],
                      there(xpair if far else dp))

    def came_over(far, yy, late, n):
        p = piece(1, core, yy, 1 - xl if far else xl, late)
        remote(p, p, ossem.at[far, n], orsem.at[far, n], there(dp)).wait_recv()

    def share(p, yy, other, late, n):
        q, m = piece(p, core, yy, 1 - xl if other else xl, late), 4 * p + 2 * other + late
        send(remote(q, q, cssem.at[m, n], csem.at[m, n], here(cpair)))

    def shared(p, yy, other, late, n):
        q, m = piece(p, 1 - core, yy, 1 - xl if other else xl, late), 4 * p + 2 * other + late
        remote(q, q, cssem.at[m, n], csem.at[m, n], here(cpair)).wait_recv()

    def split(p, cc, yy, xx, late):
        row = pl.multiple_of(((yy * 2 + xx) * 2 + cc) * ROWS, ROWS)
        base = EARLY if late else 0

        def step(m, carry):
            b = 4 * p + (2 if late else 0) + m
            for j in range(T):
                w = jnp.concatenate([G[p, cc, yy, xx, base + m * 2 * T + j], G[p, cc, yy, xx, base + m * 2 * T + T + j]], 0)
                hi = w.astype(BF16)
                lo = (w - hi.astype(F32)).astype(BF16)
                lanes = slice(128 * j, 128 * j + 128)
                W3[b, pl.ds(row, ROWS), lanes] = hi
                W3[b, pl.ds(pl.multiple_of(C + row, ROWS), ROWS), lanes] = hi
                W3[b, pl.ds(pl.multiple_of(2 * C + row, ROWS), ROWS), lanes] = lo
            return carry

        lax.fori_loop(0, 2, step, 0)

    def both(k):
        return (0,) if k in (0, half) else (0, 1)

    def from_core(p, k):
        for way in both(k):
            yy = place(way, k)
            for other in (0, 1):
                for late in (0, 1):
                    shared(p, yy, other, late, slot(way, k))
                    split(p, 1 - core, yy, 1 - xl if other else xl, late)

    def ring_step(streams, k):
        got = []
        for stream in streams:
            for way in (0, 1):
                if not carried(way, stream, k):
                    continue
                yy = arrived(way, stream, k)
                if carried(way, stream, k + 1):
                    send(ring(way, stream, k + 1))
                n = slot(way, k)
                if stream == LATE:
                    send(cross(way, k))
                p = 1 if stream >= TWIN else 0
                share(p, yy, 1 if stream in (PAIR, TWIN_PAIR) else 0, 1 if stream == LATE else 0, n)
                got.append((p, yy, column(stream), stream == LATE))
        for p, yy, xx, late in got:
            split(p, core, yy, xx, late)

    def own_tail(k):
        for way in both(k):
            crossed(way, k)
            share(0, place(way, k), 1, 1, slot(way, k))
            split(0, core, place(way, k), 1 - xl, True)
        from_core(0, k)

    def send_over(k):
        for way in both(k):
            for far in (0, 1):
                send(over(far, place(way, k), True, slot(way, k)))

    def twin_tail(k):
        for way in both(k):
            for far in (0, 1):
                yy = place(way, k)
                came_over(far, yy, True, slot(way, k))
                share(1, yy, far, 1, slot(way, k))
                split(1, core, yy, 1 - xl if far else xl, True)

    own = piece(0, core, y, xl, False)
    send(remote(own, own, xssem.at[Y], xsem.at[Y], here(xpair)))
    for stream in (OWN, LATE):
        for way in (0, 1):
            if carried(way, stream, 1):
                send(ring(way, stream, 1))
    send(cross(0, 0))
    share(0, y, 0, 0, 0)
    share(0, y, 0, 1, 0)
    for far in (0, 1):
        send(over(far, y, False, Y))
    old_copy = remote(pend.at[1], BUF.at[2], mssem.at[2, 0], mrsem.at[2, 0], at(nxt2))

    @pl.when((odd == 1) & (sec < S - 2))
    def _():
        old_copy.start()

    split(0, core, y, xl, False)
    split(0, core, y, xl, True)
    other_own = piece(0, core, y, 1 - xl, False)
    remote(other_own, other_own, xssem.at[Y], xsem.at[Y], here(xpair)).wait_recv()
    for way in (0, 1):
        if carried(way, PAIR, 1):
            send(ring(way, PAIR, 1))
    share(0, y, 1, 0, 0)
    split(0, core, y, 1 - xl, False)

    def start_twin():
        for far in (0, 1):
            came_over(far, y, False, Y)
            for way in (0, 1):
                stream = TWIN_PAIR if far else TWIN
                if carried(way, stream, 1):
                    send(ring(way, stream, 1))
            share(1, y, far, 0, 0)
            split(1, core, y, 1 - xl if far else xl, False)

    LAG = 2
    for k in range(1, half + 1):
        ring_step((LATE, OWN, PAIR), k)
        own_tail(k - 1)
        send_over(k - 1)
        if k == min(LAG, half):
            start_twin()
        if k > LAG:
            ring_step((TWIN, TWIN_PAIR), k - LAG)
    own_tail(half)
    send_over(half)

    lane = lax.broadcasted_iota(jnp.int32, (8, 128), 1) // ROWS

    def gather_taps(p):
        def step(g, carry):
            lanes = pl.ds(pl.multiple_of(g * 128, 128), 128)
            tiles = [G[p, e % 2, 2 * g + e // 4, (e // 2) % 2, EARLY - 1] for e in range(8)]
            for q in range(8):
                row = jnp.zeros((8, 128), F32)
                for e in range(8):
                    shift = ((e - q) % 8) * ROWS
                    moved = pltpu.roll(tiles[e], shift, 1) if shift else tiles[e]
                    row = jnp.where(lane == e, moved, row)
                taps[p, q, :, lanes] = row
            return carry

        lax.fori_loop(0, T, step, 0)

    gather_taps(0)
    for c in local[1:]:
        c.wait()

    @pl.when(sec == 0)
    def _():
        for c in stems_zero:
            c.wait()

    @pl.when(sec == 1)
    def _():
        for c in stems_one:
            c.wait()

    col = lax.broadcasted_iota(jnp.int32, (1, GRID, KC), 1)

    def depthwise(v, p, b, kc, acts):
        def tap(t):
            n = 9 * b + t
            return taps[p, n % 8, n // 8:n // 8 + 1, kc * KC:(kc + 1) * KC].reshape(1, 1, KC)

        v = jnp.maximum(v.reshape(GRID, GRID, KC), 0.0)
        left, right = pltpu.roll(v, 1, 1), pltpu.roll(v, GRID - 1, 1)
        rows = []
        for i in range(3):
            kl = jnp.where(col == 0, 0.0, jnp.broadcast_to(tap(3 * i), (1, GRID, KC)))
            kr = jnp.where(col == GRID - 1, 0.0, jnp.broadcast_to(tap(3 * i + 2), (1, GRID, KC)))
            rows.append(left * kl + v * tap(3 * i + 1) + right * kr)
        zero = jnp.zeros((1, GRID, KC), F32)
        total = (jnp.concatenate([zero, rows[0][:GRID - 1]], 0) + rows[1]
                 + jnp.concatenate([rows[2][1:], zero], 0)).reshape(PIX, KC)
        hi = total.astype(BF16)
        lo = (total - hi.astype(F32)).astype(BF16)
        acts[:, kc * KC:(kc + 1) * KC] = hi
        acts[:, C + kc * KC:C + (kc + 1) * KC] = lo
        acts[:, 2 * C + kc * KC:2 * C + (kc + 1) * KC] = hi

    part = lambda nc: slice(nc * KC, (nc + 1) * KC)
    span = lambda nc: pl.ds(nc * KC, KC)

    def landed(m, nc):
        r = BUF.at[m, :, span(nc)]
        remote(r, r, mssem.at[m, nc], mrsem.at[m, nc], at(prv)).wait_recv()

    def pass_on(t, m, nc, dev):
        return remote(BUF.at[8 + t, :, span(nc)], BUF.at[m, :, span(nc)], mssem.at[m, nc], mrsem.at[m, nc], dev)

    up0 = lambda nc: pass_on(0, 4 - odd, nc, at(nxt2))
    up1 = lambda nc: pass_on(1, 5, nc, at(nxt2))
    up2 = lambda nc: pass_on(2, 7, nc, at(nxt))
    home = remote(BUF.at[9], OUT.at[1], mssem.at[8, 0], mrsem.at[8, 0], there(dp))
    again = lambda nc: remote(OUT.at[1, :, span(nc)], BUF.at[6, :, span(nc)], mssem.at[6, nc], mrsem.at[6, nc], at(nxt2))
    aside = remote(BUF.at[5, :, span(1)], BUF.at[6, :, span(1)], mssem.at[8, 1], mrsem.at[6, 1], there(dp))

    def cell(t, p):
        ear = jnp.where(t == 0, 0, jnp.where(t == 1, 1 + odd, jnp.where(t == 2, 4 - odd, 6)))
        new = jnp.where(t == 0, 1, jnp.where(t == 1, 8 - 5 * odd, jnp.where(t == 2, 5 + 4 * odd, 7)))

        def product(acts, b, nc):
            return jnp.dot(acts[...], W3[4 * p + b, :, nc * KC:(nc + 1) * KC], preferred_element_type=F32)

        @pl.when((t == 1) & (odd == 1) & (sec > 1))
        def _():
            r = BUF.at[2]
            remote(r, r, mssem.at[2, 0], mrsem.at[2, 0], at(prv2)).wait_recv()

        @pl.when((t == 2) & (odd == 0) & (sec > 1))
        def _():
            landed(4, 0)
            landed(4, 1)

        @pl.when((t == 3) & (sec > 1))
        def _():
            landed(6, 0)
            landed(6, 1)

        for kc in (0, 1):
            depthwise(BUF[ear, :, part(kc)], p, 1, kc, B3)
        for nc in (0, 1):
            first[:, part(nc)] = product(B3, 1, nc)
        for kc in (0, 1):
            @pl.when((t == 1) & (odd == 1) & (sec > 1))
            def _():
                landed(3, kc)

            @pl.when((t == 2) & (odd == 0) & (sec > 1))
            def _():
                landed(5, kc)
                if kc == 1:
                    aside.start()

            @pl.when((t == 3) & (sec > 0))
            def _():
                landed(7, kc)

            depthwise(BUF[new, :, part(kc)], p, 0, kc, A3)
        for nc in (0, 1):
            first[:, part(nc)] += product(A3, 0, nc)
        for kc in (0, 1):
            depthwise(first[:, part(kc)], p, 2, kc, B3)
        for nc in (0, 1):
            second[:, part(nc)] = product(B3, 2, nc) + BUF[new, :, part(nc)]
        for kc in (0, 1):
            depthwise(second[:, part(kc)], p, 3, kc, A3)
        for nc in (0, 1):
            v = product(A3, 3, nc) + first[:, part(nc)]
            BUF[8 + t, :, part(nc)] = v

            @pl.when(t != 1)
            def _():
                OUT[t, :, part(nc)] = v

            @pl.when((t == 0) & (sec < S - 2))
            def _():
                up0(nc).start()

            @pl.when((t == 1) & (odd == 0) & (sec < S - 2))
            def _():
                up1(nc).start()

            if nc == 0:
                @pl.when(t == 2)
                def _():
                    home.wait_send()

            @pl.when((t == 2) & (sec < S - 1))
            def _():
                up2(nc).start()

        @pl.when(t == 1)
        def _():
            home.start()

        @pl.when(t == 2)
        def _():
            home.wait_recv()

        @pl.when((t == 2) & (sec < S - 2))
        def _():
            again(0).start()

        @pl.when((t == 2) & (odd == 0) & (sec < S - 2))
        def _():
            again(1).start()

    cell(jnp.int32(0), 0)

    for k in range(max(half - LAG, 0) + 1, half + 1):
        ring_step((TWIN, TWIN_PAIR), k)
    for k in range(half + 1):
        twin_tail(k)
    for k in range(half + 1):
        from_core(1, k)
    gather_taps(1)

    def tick(t, carry):
        cell(t, jnp.where(t == 1, 1, 0))
        return carry

    lax.fori_loop(1, TICKS, tick, 0)

    for c in sent:
        c.wait_send()

    @pl.when((odd == 1) & (sec < S - 2))
    def _():
        old_copy.wait_send()

    @pl.when(sec < S - 2)
    def _():
        for nc in (0, 1):
            up0(nc).wait_send()
        again(0).wait_send()

    @pl.when((odd == 0) & (sec > 1))
    def _():
        aside.wait_send()

    @pl.when((odd == 0) & (sec < S - 2))
    def _():
        again(1).wait_send()
        for nc in (0, 1):
            up1(nc).wait_send()

    @pl.when(sec < S - 1)
    def _():
        for nc in (0, 1):
            up2(nc).wait_send()


def body(S, Y, pend, stem, spatial, mixing):
    C = mixing.shape[-1]
    T = C // 128
    pend = pend.reshape(2, PIX, C)
    stem = stem.reshape(TICKS - 1, PIX, C)
    flat = jnp.pad(spatial.reshape(36, ROWS), ((0, 28), (0, 0))).reshape(1, 8, 128)
    tiles = mixing.reshape(4, 2, 8, T, 128).transpose(0, 1, 3, 2, 4).reshape(8 * T, 8, 128)
    blk = jnp.concatenate([tiles[:4 * T], flat, tiles[4 * T:]], 0)
    dma = pltpu.SemaphoreType.DMA
    any_ = pl.BlockSpec(memory_space=pl.ANY)
    half = Y // 2
    out = pl.pallas_call(
        functools.partial(kernel, S, Y, C),
        out_shape=jax.ShapeDtypeStruct((TICKS, PIX, C), F32),
        in_specs=[any_] * 3,
        out_specs=pl.BlockSpec(memory_space=pltpu.VMEM),
        scratch_shapes=[
            pltpu.VMEM((2, 2, Y, 2, 8 * T + 1, 8, 128), F32),
            pltpu.VMEM((8, 3 * C, C), BF16),
            pltpu.VMEM((PIX, 3 * C), BF16),
            pltpu.VMEM((PIX, 3 * C), BF16),
            pltpu.VMEM((2, 8, 8, C), F32),
            pltpu.VMEM((12, PIX, C), F32),
            pltpu.VMEM((PIX, C), F32),
            pltpu.VMEM((PIX, C), F32),
            dma((13,)),
            dma((2, 5, half)),
            dma((2, 5, half)),
            dma((Y + 1,)),
            dma((Y + 1,)),
            dma((2, Y + 1)),
            dma((2, Y + 1)),
            dma((8, Y)),
            dma((8, Y)),
            dma((9, 2)),
            dma((9, 2)),
        ],
        compiler_params=pltpu.CompilerParams(collective_id=0, has_side_effects=True, vmem_limit_bytes=38 << 20),
        name="relay",
    )(pend, stem, blk)
    return out.reshape(1, TICKS, 1, GRID, GRID, C)


def solution(mesh):
    S, D = mesh.shape["section"], mesh.shape["dp"]
    placed = (
        P("section", None, "dp", None, None, None),
        P(None, "dp", None, None, None),
        P("section", None, None, "dp"),
        P("section", None, "dp", None),
    )
    return jax.shard_map(
        functools.partial(body, S, D // 4),
        mesh=mesh,
        in_specs=placed,
        out_specs=P("section", None, "dp", None, None, None),
        check_vma=False,
    )
```

```python
import functools

import jax
import jax.numpy as jnp
from jax import lax
from jax.experimental import pallas as pl
from jax.experimental.pallas import tpu as pltpu
from jax.sharding import PartitionSpec as P

MESH = pl.DeviceIdType.MESH
F32, BF16 = jnp.float32, jnp.bfloat16
GRID = 16
PIX = GRID * GRID
TICKS = 4
ROWS = 16
OWN, PAIR, LATE, TWIN, TWIN_PAIR = range(5)


def kernel(S, Y, C, pend, stem, blk, OUT, G, W3, A3, B3, taps, BUF, first, second,
           lsem, ssem, rsem, xssem, xsem, ossem, orsem, cssem, csem, mssem, mrsem):
    D = Y * 4
    T = C // 128
    EARLY, ALL = 4 * T + 1, 8 * T + 1
    KC = C // 2
    half = Y // 2
    sec, dp = lax.axis_index("section"), lax.axis_index("dp")
    odd = lax.rem(sec, 2)
    y, xl, core = dp // 4, lax.rem(dp // 2, 2), lax.rem(dp, 2)
    yup, ydn = lax.rem(dp + 4, D), lax.rem(dp + D - 4, D)
    xpair, cpair = dp + 2 - 4 * xl, dp + 1 - 2 * core
    twin = sec + 1 - 2 * odd
    here = lambda d: {"section": sec, "dp": d}
    at = lambda s: {"section": s, "dp": dp}
    there = lambda d: {"section": twin, "dp": d}
    nxt, nxt2 = lax.rem(sec + 1, S), lax.rem(sec + 2, S)
    prv, prv2 = lax.rem(sec + S - 1, S), lax.rem(sec + S - 2, S)

    local = [
        pltpu.make_async_copy(blk, G.at[0, core, y, xl], lsem.at[0]),
        pltpu.make_async_copy(pend.at[0], BUF.at[0], lsem.at[1]),
        pltpu.make_async_copy(pend.at[1], BUF.at[1], lsem.at[2]),
    ]
    for c in local:
        c.start()
    stems_zero = [pltpu.make_async_copy(stem.at[n], BUF.at[m], lsem.at[m]) for n, m in ((1, 4), (1, 5), (2, 6), (2, 7))]
    stems_one = [pltpu.make_async_copy(stem.at[n], BUF.at[m], lsem.at[m + 6]) for n, m in ((0, 2), (0, 3), (1, 6))]

    @pl.when(sec == 0)
    def _():
        for c in stems_zero:
            c.start()

    @pl.when(sec == 1)
    def _():
        for c in stems_one:
            c.start()

    barrier = pltpu.get_barrier_semaphore()
    partners = (here(yup), here(ydn), here(xpair), here(cpair), there(dp), there(xpair), at(nxt), at(prv), at(nxt2), at(prv2))
    for d in partners:
        pl.semaphore_signal(barrier, inc=1, device_id=d, device_id_type=MESH)
    pl.semaphore_wait(barrier, len(partners))
    local[0].wait()

    sent = []

    def remote(src, dst, s, r, dev):
        return pltpu.make_async_remote_copy(src_ref=src, dst_ref=dst, send_sem=s, recv_sem=r,
                                            device_id=dev, device_id_type=MESH)

    def send(c):
        c.start()
        sent.append(c)

    def piece(p, cc, yy, xx, late):
        lo, n = (EARLY, ALL - EARLY) if late else (0, EARLY)
        return G.at[p, cc, yy, xx, pl.ds(lo, n)]

    def column(stream):
        return xl if stream in (OWN, LATE, TWIN) else 1 - xl

    def place(way, k):
        return lax.rem(y + Y - k, Y) if way == 0 else lax.rem(y + k, Y)

    def ring_piece(stream, yy):
        return piece(1 if stream >= TWIN else 0, core, yy, column(stream), stream == LATE)

    def ring(way, stream, k):
        p = ring_piece(stream, place(way, k - 1))
        return remote(p, p, ssem.at[way, stream, k - 1], rsem.at[way, stream, k - 1], here(yup if way == 0 else ydn))

    def carried(way, stream, k):
        return k < half or (k == half and way == (1 if stream in (PAIR, TWIN_PAIR) else 0))

    def arrived(way, stream, k):
        yy = place(way, k)
        p = ring_piece(stream, yy)
        remote(p, p, ssem.at[way, stream, k - 1], rsem.at[way, stream, k - 1], here(ydn)).wait_recv()
        return yy

    def slot(way, k):
        return 0 if k == 0 else (k if way == 0 else Y - k)

    def cross(way, k):
        p = piece(0, core, place(way, k), xl, True)
        return remote(p, p, xssem.at[slot(way, k)], xsem.at[slot(way, k)], here(xpair))

    def crossed(way, k):
        p = piece(0, core, place(way, k), 1 - xl, True)
        remote(p, p, xssem.at[slot(way, k)], xsem.at[slot(way, k)], here(xpair)).wait_recv()

    def over(far, yy, late, n):
        return remote(piece(0, core, yy, xl, late), piece(1, core, yy, xl, late), ossem.at[far, n], orsem.at[far, n],
                      there(xpair if far else dp))

    def came_over(far, yy, late, n):
        p = piece(1, core, yy, 1 - xl if far else xl, late)
        remote(p, p, ossem.at[far, n], orsem.at[far, n], there(dp)).wait_recv()

    def share(p, yy, other, late, n):
        q, m = piece(p, core, yy, 1 - xl if other else xl, late), 4 * p + 2 * other + late
        send(remote(q, q, cssem.at[m, n], csem.at[m, n], here(cpair)))

    def shared(p, yy, other, late, n):
        q, m = piece(p, 1 - core, yy, 1 - xl if other else xl, late), 4 * p + 2 * other + late
        remote(q, q, cssem.at[m, n], csem.at[m, n], here(cpair)).wait_recv()

    def split(p, cc, yy, xx, late):
        row = pl.multiple_of(((yy * 2 + xx) * 2 + cc) * ROWS, ROWS)
        base = EARLY if late else 0

        def step(m, carry):
            b = 4 * p + (2 if late else 0) + m
            for j in range(T):
                w = jnp.concatenate([G[p, cc, yy, xx, base + m * 2 * T + j], G[p, cc, yy, xx, base + m * 2 * T + T + j]], 0)
                hi = w.astype(BF16)
                lo = (w - hi.astype(F32)).astype(BF16)
                lanes = slice(128 * j, 128 * j + 128)
                W3[b, pl.ds(row, ROWS), lanes] = hi
                W3[b, pl.ds(pl.multiple_of(C + row, ROWS), ROWS), lanes] = hi
                W3[b, pl.ds(pl.multiple_of(2 * C + row, ROWS), ROWS), lanes] = lo
            return carry

        lax.fori_loop(0, 2, step, 0)

    def both(k):
        return (0,) if k in (0, half) else (0, 1)

    def from_core(p, k):
        for way in both(k):
            yy = place(way, k)
            for other in (0, 1):
                for late in (0, 1):
                    shared(p, yy, other, late, slot(way, k))
                    split(p, 1 - core, yy, 1 - xl if other else xl, late)

    def ring_step(streams, k):
        got = []
        for stream in streams:
            for way in (0, 1):
                if not carried(way, stream, k):
                    continue
                yy = arrived(way, stream, k)
                if carried(way, stream, k + 1):
                    send(ring(way, stream, k + 1))
                n = slot(way, k)
                if stream == LATE:
                    send(cross(way, k))
                p = 1 if stream >= TWIN else 0
                share(p, yy, 1 if stream in (PAIR, TWIN_PAIR) else 0, 1 if stream == LATE else 0, n)
                got.append((p, yy, column(stream), stream == LATE))
        for p, yy, xx, late in got:
            split(p, core, yy, xx, late)

    def own_tail(k):
        for way in both(k):
            crossed(way, k)
            share(0, place(way, k), 1, 1, slot(way, k))
            split(0, core, place(way, k), 1 - xl, True)
        from_core(0, k)

    def send_over(k):
        for way in both(k):
            for far in (0, 1):
                send(over(far, place(way, k), True, slot(way, k)))

    def twin_tail(k):
        for way in both(k):
            for far in (0, 1):
                yy = place(way, k)
                came_over(far, yy, True, slot(way, k))
                share(1, yy, far, 1, slot(way, k))
                split(1, core, yy, 1 - xl if far else xl, True)

    own = piece(0, core, y, xl, False)
    send(remote(own, own, xssem.at[Y], xsem.at[Y], here(xpair)))
    for stream in (OWN, LATE):
        for way in (0, 1):
            if carried(way, stream, 1):
                send(ring(way, stream, 1))
    send(cross(0, 0))
    share(0, y, 0, 0, 0)
    share(0, y, 0, 1, 0)
    for far in (0, 1):
        send(over(far, y, False, Y))
    old_copy = remote(pend.at[1], BUF.at[2], mssem.at[2, 0], mrsem.at[2, 0], at(nxt2))

    @pl.when((odd == 1) & (sec < S - 2))
    def _():
        old_copy.start()

    split(0, core, y, xl, False)
    split(0, core, y, xl, True)
    other_own = piece(0, core, y, 1 - xl, False)
    remote(other_own, other_own, xssem.at[Y], xsem.at[Y], here(xpair)).wait_recv()
    for way in (0, 1):
        if carried(way, PAIR, 1):
            send(ring(way, PAIR, 1))
    share(0, y, 1, 0, 0)
    split(0, core, y, 1 - xl, False)

    def start_twin():
        for far in (0, 1):
            came_over(far, y, False, Y)
            for way in (0, 1):
                stream = TWIN_PAIR if far else TWIN
                if carried(way, stream, 1):
                    send(ring(way, stream, 1))
            share(1, y, far, 0, 0)
            split(1, core, y, 1 - xl if far else xl, False)

    LAG = 2
    for k in range(1, half + 1):
        ring_step((LATE, OWN, PAIR), k)
        own_tail(k - 1)
        send_over(k - 1)
        if k == min(LAG, half):
            start_twin()
        if k > LAG:
            ring_step((TWIN, TWIN_PAIR), k - LAG)
    own_tail(half)
    send_over(half)

    lane = lax.broadcasted_iota(jnp.int32, (8, 128), 1) // ROWS

    def gather_taps(p):
        def step(g, carry):
            lanes = pl.ds(pl.multiple_of(g * 128, 128), 128)
            tiles = [G[p, e % 2, 2 * g + e // 4, (e // 2) % 2, EARLY - 1] for e in range(8)]
            for q in range(8):
                row = jnp.zeros((8, 128), F32)
                for e in range(8):
                    shift = ((e - q) % 8) * ROWS
                    moved = pltpu.roll(tiles[e], shift, 1) if shift else tiles[e]
                    row = jnp.where(lane == e, moved, row)
                taps[p, q, :, lanes] = row
            return carry

        lax.fori_loop(0, T, step, 0)

    gather_taps(0)
    for c in local[1:]:
        c.wait()

    @pl.when(sec == 0)
    def _():
        for c in stems_zero:
            c.wait()

    @pl.when(sec == 1)
    def _():
        for c in stems_one:
            c.wait()

    col = lax.broadcasted_iota(jnp.int32, (1, GRID, KC), 1)

    def depthwise(v, p, b, kc, acts):
        def tap(t):
            n = 9 * b + t
            return taps[p, n % 8, n // 8:n // 8 + 1, kc * KC:(kc + 1) * KC].reshape(1, 1, KC)

        v = jnp.maximum(v.reshape(GRID, GRID, KC), 0.0)
        left, right = pltpu.roll(v, 1, 1), pltpu.roll(v, GRID - 1, 1)
        rows = []
        for i in range(3):
            kl = jnp.where(col == 0, 0.0, jnp.broadcast_to(tap(3 * i), (1, GRID, KC)))
            kr = jnp.where(col == GRID - 1, 0.0, jnp.broadcast_to(tap(3 * i + 2), (1, GRID, KC)))
            rows.append(left * kl + v * tap(3 * i + 1) + right * kr)
        zero = jnp.zeros((1, GRID, KC), F32)
        total = (jnp.concatenate([zero, rows[0][:GRID - 1]], 0) + rows[1]
                 + jnp.concatenate([rows[2][1:], zero], 0)).reshape(PIX, KC)
        hi = total.astype(BF16)
        lo = (total - hi.astype(F32)).astype(BF16)
        acts[:, kc * KC:(kc + 1) * KC] = hi
        acts[:, C + kc * KC:C + (kc + 1) * KC] = lo
        acts[:, 2 * C + kc * KC:2 * C + (kc + 1) * KC] = hi

    part = lambda nc: slice(nc * KC, (nc + 1) * KC)
    span = lambda nc: pl.ds(nc * KC, KC)

    def landed(m, nc):
        r = BUF.at[m, :, span(nc)]
        remote(r, r, mssem.at[m, nc], mrsem.at[m, nc], at(prv)).wait_recv()

    def pass_on(t, m, nc, dev):
        return remote(BUF.at[8 + t, :, span(nc)], BUF.at[m, :, span(nc)], mssem.at[m, nc], mrsem.at[m, nc], dev)

    up0 = lambda nc: pass_on(0, 4 - odd, nc, at(nxt2))
    up1 = lambda nc: pass_on(1, 5, nc, at(nxt2))
    up2 = lambda nc: pass_on(2, 7, nc, at(nxt))
    home = remote(BUF.at[9], OUT.at[1], mssem.at[8, 0], mrsem.at[8, 0], there(dp))
    again = lambda nc: remote(OUT.at[1, :, span(nc)], BUF.at[6, :, span(nc)], mssem.at[6, nc], mrsem.at[6, nc], at(nxt2))
    aside = remote(BUF.at[5, :, span(1)], BUF.at[6, :, span(1)], mssem.at[8, 1], mrsem.at[6, 1], there(dp))

    def cell(t, p):
        ear = jnp.where(t == 0, 0, jnp.where(t == 1, 1 + odd, jnp.where(t == 2, 4 - odd, 6)))
        new = jnp.where(t == 0, 1, jnp.where(t == 1, 8 - 5 * odd, jnp.where(t == 2, 5 + 4 * odd, 7)))

        def product(acts, b, nc):
            return jnp.dot(acts[...], W3[4 * p + b, :, nc * KC:(nc + 1) * KC], preferred_element_type=F32)

        @pl.when((t == 1) & (odd == 1) & (sec > 1))
        def _():
            r = BUF.at[2]
            remote(r, r, mssem.at[2, 0], mrsem.at[2, 0], at(prv2)).wait_recv()

        @pl.when((t == 2) & (sec < 2))
        def _():
            home.wait_recv()

        @pl.when((t == 2) & (odd == 0) & (sec > 1))
        def _():
            landed(4, 0)
            landed(4, 1)

        @pl.when((t == 3) & (sec > 1))
        def _():
            landed(6, 0)
            landed(6, 1)

        for kc in (0, 1):
            depthwise(BUF[ear, :, part(kc)], p, 1, kc, B3)
        for nc in (0, 1):
            first[:, part(nc)] = product(B3, 1, nc)
        for kc in (0, 1):
            @pl.when((t == 1) & (odd == 1) & (sec > 1))
            def _():
                landed(3, kc)

            @pl.when((t == 2) & (odd == 0) & (sec > 1))
            def _():
                landed(5, kc)
                if kc == 1:
                    aside.start()

            @pl.when((t == 3) & (sec > 0))
            def _():
                landed(7, kc)

            depthwise(BUF[new, :, part(kc)], p, 0, kc, A3)
        for nc in (0, 1):
            first[:, part(nc)] += product(A3, 0, nc)
        for kc in (0, 1):
            depthwise(first[:, part(kc)], p, 2, kc, B3)
        for nc in (0, 1):
            second[:, part(nc)] = product(B3, 2, nc) + BUF[new, :, part(nc)]
        for kc in (0, 1):
            depthwise(second[:, part(kc)], p, 3, kc, A3)
        for nc in (0, 1):
            v = product(A3, 3, nc) + first[:, part(nc)]
            BUF[8 + t, :, part(nc)] = v

            @pl.when(t != 1)
            def _():
                OUT[t, :, part(nc)] = v

            @pl.when((t == 0) & (sec < S - 2))
            def _():
                up0(nc).start()

            @pl.when((t == 1) & (odd == 0) & (sec < S - 2))
            def _():
                up1(nc).start()

            if nc == 0:
                @pl.when(t == 2)
                def _():
                    home.wait_send()

            @pl.when((t == 2) & (sec < S - 1))
            def _():
                up2(nc).start()

        @pl.when(t == 1)
        def _():
            home.start()

        @pl.when((t == 2) & (sec > 1))
        def _():
            home.wait_recv()

        @pl.when((t == 2) & (sec < S - 2))
        def _():
            again(0).start()

        @pl.when((t == 2) & (odd == 0) & (sec < S - 2))
        def _():
            again(1).start()

    cell(jnp.int32(0), 0)

    for k in range(max(half - LAG, 0) + 1, half + 1):
        ring_step((TWIN, TWIN_PAIR), k)
    for k in range(half + 1):
        twin_tail(k)
    for k in range(half + 1):
        from_core(1, k)
    gather_taps(1)

    def tick(t, carry):
        cell(t, jnp.where(t == 1, 1, 0))
        return carry

    lax.fori_loop(1, TICKS, tick, 0)

    for c in sent:
        c.wait_send()

    @pl.when((odd == 1) & (sec < S - 2))
    def _():
        old_copy.wait_send()

    @pl.when(sec < S - 2)
    def _():
        for nc in (0, 1):
            up0(nc).wait_send()
        again(0).wait_send()

    @pl.when((odd == 0) & (sec > 1))
    def _():
        aside.wait_send()

    @pl.when((odd == 0) & (sec < S - 2))
    def _():
        again(1).wait_send()
        for nc in (0, 1):
            up1(nc).wait_send()

    @pl.when(sec < S - 1)
    def _():
        for nc in (0, 1):
            up2(nc).wait_send()


def body(S, Y, pend, stem, spatial, mixing):
    C = mixing.shape[-1]
    T = C // 128
    pend = pend.reshape(2, PIX, C)
    stem = stem.reshape(TICKS - 1, PIX, C)
    flat = jnp.pad(spatial.reshape(36, ROWS), ((0, 28), (0, 0))).reshape(1, 8, 128)
    tiles = mixing.reshape(4, 2, 8, T, 128).transpose(0, 1, 3, 2, 4).reshape(8 * T, 8, 128)
    blk = jnp.concatenate([tiles[:4 * T], flat, tiles[4 * T:]], 0)
    dma = pltpu.SemaphoreType.DMA
    any_ = pl.BlockSpec(memory_space=pl.ANY)
    half = Y // 2
    out = pl.pallas_call(
        functools.partial(kernel, S, Y, C),
        out_shape=jax.ShapeDtypeStruct((TICKS, PIX, C), F32),
        in_specs=[any_] * 3,
        out_specs=pl.BlockSpec(memory_space=pltpu.VMEM),
        scratch_shapes=[
            pltpu.VMEM((2, 2, Y, 2, 8 * T + 1, 8, 128), F32),
            pltpu.VMEM((8, 3 * C, C), BF16),
            pltpu.VMEM((PIX, 3 * C), BF16),
            pltpu.VMEM((PIX, 3 * C), BF16),
            pltpu.VMEM((2, 8, 8, C), F32),
            pltpu.VMEM((12, PIX, C), F32),
            pltpu.VMEM((PIX, C), F32),
            pltpu.VMEM((PIX, C), F32),
            dma((13,)),
            dma((2, 5, half)),
            dma((2, 5, half)),
            dma((Y + 1,)),
            dma((Y + 1,)),
            dma((2, Y + 1)),
            dma((2, Y + 1)),
            dma((8, Y)),
            dma((8, Y)),
            dma((9, 2)),
            dma((9, 2)),
        ],
        compiler_params=pltpu.CompilerParams(collective_id=0, has_side_effects=True, vmem_limit_bytes=38 << 20),
        name="relay",
    )(pend, stem, blk)
    return out.reshape(1, TICKS, 1, GRID, GRID, C)


def solution(mesh):
    S, D = mesh.shape["section"], mesh.shape["dp"]
    placed = (
        P("section", None, "dp", None, None, None),
        P(None, "dp", None, None, None),
        P("section", None, None, "dp"),
        P("section", None, "dp", None),
    )
    return jax.shard_map(
        functools.partial(body, S, D // 4),
        mesh=mesh,
        in_specs=placed,
        out_specs=P("section", None, "dp", None, None, None),
        check_vma=False,
    )
```

```python
import functools

import jax
import jax.numpy as jnp
from jax import lax
from jax.experimental import pallas as pl
from jax.experimental.pallas import tpu as pltpu
from jax.sharding import PartitionSpec as P

MESH = pl.DeviceIdType.MESH
F32, BF16 = jnp.float32, jnp.bfloat16
GRID = 16
PIX = GRID * GRID
TICKS = 4
ROWS = 16
OWN, PAIR, LATE, TWIN, TWIN_PAIR = range(5)


def kernel(S, Y, C, pend, stem, blk, OUT, G, W3, A3, B3, taps, BUF, first, second,
           lsem, ssem, rsem, xssem, xsem, ossem, orsem, cssem, csem, mssem, mrsem):
    D = Y * 4
    T = C // 128
    EARLY, ALL = 4 * T + 1, 8 * T + 1
    KC = C // 2
    half = Y // 2
    sec, dp = lax.axis_index("section"), lax.axis_index("dp")
    odd = lax.rem(sec, 2)
    y, xl, core = dp // 4, lax.rem(dp // 2, 2), lax.rem(dp, 2)
    yup, ydn = lax.rem(dp + 4, D), lax.rem(dp + D - 4, D)
    xpair, cpair = dp + 2 - 4 * xl, dp + 1 - 2 * core
    twin = sec + 1 - 2 * odd
    here = lambda d: {"section": sec, "dp": d}
    at = lambda s: {"section": s, "dp": dp}
    there = lambda d: {"section": twin, "dp": d}
    nxt, nxt2 = lax.rem(sec + 1, S), lax.rem(sec + 2, S)
    prv, prv2 = lax.rem(sec + S - 1, S), lax.rem(sec + S - 2, S)

    local = [
        pltpu.make_async_copy(blk, G.at[0, core, y, xl], lsem.at[0]),
        pltpu.make_async_copy(pend.at[0], BUF.at[0], lsem.at[1]),
        pltpu.make_async_copy(pend.at[1], BUF.at[1], lsem.at[2]),
    ]
    for c in local:
        c.start()
    stems_zero = [pltpu.make_async_copy(stem.at[n], BUF.at[m], lsem.at[m]) for n, m in ((1, 4), (1, 5), (2, 6), (2, 7))]
    stems_one = [pltpu.make_async_copy(stem.at[n], BUF.at[m], lsem.at[m + 6]) for n, m in ((0, 2), (0, 3), (1, 6))]

    @pl.when(sec == 0)
    def _():
        for c in stems_zero:
            c.start()

    @pl.when(sec == 1)
    def _():
        for c in stems_one:
            c.start()

    barrier = pltpu.get_barrier_semaphore()
    partners = (here(yup), here(ydn), here(xpair), here(cpair), there(dp), there(xpair), at(nxt), at(prv), at(nxt2), at(prv2))
    for d in partners:
        pl.semaphore_signal(barrier, inc=1, device_id=d, device_id_type=MESH)
    pl.semaphore_wait(barrier, len(partners))
    local[0].wait()

    sent = []

    def remote(src, dst, s, r, dev):
        return pltpu.make_async_remote_copy(src_ref=src, dst_ref=dst, send_sem=s, recv_sem=r,
                                            device_id=dev, device_id_type=MESH)

    def send(c):
        c.start()
        sent.append(c)

    def piece(p, cc, yy, xx, late):
        lo, n = (EARLY, ALL - EARLY) if late else (0, EARLY)
        return G.at[p, cc, yy, xx, pl.ds(lo, n)]

    def column(stream):
        return xl if stream in (OWN, LATE, TWIN) else 1 - xl

    def place(way, k):
        return lax.rem(y + Y - k, Y) if way == 0 else lax.rem(y + k, Y)

    def ring_piece(stream, yy):
        return piece(1 if stream >= TWIN else 0, core, yy, column(stream), stream == LATE)

    def ring(way, stream, k):
        p = ring_piece(stream, place(way, k - 1))
        return remote(p, p, ssem.at[way, stream, k - 1], rsem.at[way, stream, k - 1], here(yup if way == 0 else ydn))

    def carried(way, stream, k):
        return k < half or (k == half and way == (1 if stream in (PAIR, TWIN_PAIR) else 0))

    def arrived(way, stream, k):
        yy = place(way, k)
        p = ring_piece(stream, yy)
        remote(p, p, ssem.at[way, stream, k - 1], rsem.at[way, stream, k - 1], here(ydn)).wait_recv()
        return yy

    def slot(way, k):
        return 0 if k == 0 else (k if way == 0 else Y - k)

    def cross(way, k):
        p = piece(0, core, place(way, k), xl, True)
        return remote(p, p, xssem.at[slot(way, k)], xsem.at[slot(way, k)], here(xpair))

    def crossed(way, k):
        p = piece(0, core, place(way, k), 1 - xl, True)
        remote(p, p, xssem.at[slot(way, k)], xsem.at[slot(way, k)], here(xpair)).wait_recv()

    def over(far, yy, late, n):
        return remote(piece(0, core, yy, xl, late), piece(1, core, yy, xl, late), ossem.at[far, n], orsem.at[far, n],
                      there(xpair if far else dp))

    def came_over(far, yy, late, n):
        p = piece(1, core, yy, 1 - xl if far else xl, late)
        remote(p, p, ossem.at[far, n], orsem.at[far, n], there(dp)).wait_recv()

    def share(p, yy, other, late, n):
        q, m = piece(p, core, yy, 1 - xl if other else xl, late), 4 * p + 2 * other + late
        send(remote(q, q, cssem.at[m, n], csem.at[m, n], here(cpair)))

    def shared(p, yy, other, late, n):
        q, m = piece(p, 1 - core, yy, 1 - xl if other else xl, late), 4 * p + 2 * other + late
        remote(q, q, cssem.at[m, n], csem.at[m, n], here(cpair)).wait_recv()

    def split(p, cc, yy, xx, late):
        row = pl.multiple_of(((yy * 2 + xx) * 2 + cc) * ROWS, ROWS)
        base = EARLY if late else 0

        def step(m, carry):
            b = 4 * p + (2 if late else 0) + m
            for j in range(T):
                w = jnp.concatenate([G[p, cc, yy, xx, base + m * 2 * T + j], G[p, cc, yy, xx, base + m * 2 * T + T + j]], 0)
                hi = w.astype(BF16)
                lo = (w - hi.astype(F32)).astype(BF16)
                lanes = slice(128 * j, 128 * j + 128)
                W3[b, pl.ds(row, ROWS), lanes] = hi
                W3[b, pl.ds(pl.multiple_of(C + row, ROWS), ROWS), lanes] = hi
                W3[b, pl.ds(pl.multiple_of(2 * C + row, ROWS), ROWS), lanes] = lo
            return carry

        lax.fori_loop(0, 2, step, 0)

    def both(k):
        return (0,) if k in (0, half) else (0, 1)

    def from_core(p, k):
        for way in both(k):
            yy = place(way, k)
            for other in (0, 1):
                for late in (0, 1):
                    shared(p, yy, other, late, slot(way, k))
                    split(p, 1 - core, yy, 1 - xl if other else xl, late)

    def ring_step(streams, k):
        got = []
        for stream in streams:
            for way in (0, 1):
                if not carried(way, stream, k):
                    continue
                yy = arrived(way, stream, k)
                if carried(way, stream, k + 1):
                    send(ring(way, stream, k + 1))
                n = slot(way, k)
                if stream == LATE:
                    send(cross(way, k))
                p = 1 if stream >= TWIN else 0
                share(p, yy, 1 if stream in (PAIR, TWIN_PAIR) else 0, 1 if stream == LATE else 0, n)
                got.append((p, yy, column(stream), stream == LATE))
        for p, yy, xx, late in got:
            split(p, core, yy, xx, late)

    def own_tail(k):
        for way in both(k):
            crossed(way, k)
            share(0, place(way, k), 1, 1, slot(way, k))
            split(0, core, place(way, k), 1 - xl, True)
        from_core(0, k)

    def send_over(k):
        for way in both(k):
            for far in (0, 1):
                send(over(far, place(way, k), True, slot(way, k)))

    def twin_tail(k):
        for way in both(k):
            for far in (0, 1):
                yy = place(way, k)
                came_over(far, yy, True, slot(way, k))
                share(1, yy, far, 1, slot(way, k))
                split(1, core, yy, 1 - xl if far else xl, True)

    own = piece(0, core, y, xl, False)
    send(remote(own, own, xssem.at[Y], xsem.at[Y], here(xpair)))
    for stream in (OWN, LATE):
        for way in (0, 1):
            if carried(way, stream, 1):
                send(ring(way, stream, 1))
    send(cross(0, 0))
    share(0, y, 0, 0, 0)
    share(0, y, 0, 1, 0)
    for far in (0, 1):
        send(over(far, y, False, Y))
    old_copy = remote(pend.at[1], BUF.at[2], mssem.at[2, 0], mrsem.at[2, 0], at(nxt2))

    @pl.when((odd == 1) & (sec < S - 2))
    def _():
        old_copy.start()

    split(0, core, y, xl, False)
    split(0, core, y, xl, True)
    other_own = piece(0, core, y, 1 - xl, False)
    remote(other_own, other_own, xssem.at[Y], xsem.at[Y], here(xpair)).wait_recv()
    for way in (0, 1):
        if carried(way, PAIR, 1):
            send(ring(way, PAIR, 1))
    share(0, y, 1, 0, 0)
    split(0, core, y, 1 - xl, False)

    def start_twin():
        for far in (0, 1):
            came_over(far, y, False, Y)
            for way in (0, 1):
                stream = TWIN_PAIR if far else TWIN
                if carried(way, stream, 1):
                    send(ring(way, stream, 1))
            share(1, y, far, 0, 0)
            split(1, core, y, 1 - xl if far else xl, False)

    LAG = 2
    for k in range(1, half + 1):
        ring_step((LATE, OWN, PAIR), k)
        own_tail(k - 1)
        send_over(k - 1)
        if k == min(LAG, half):
            start_twin()
        if k > LAG:
            ring_step((TWIN, TWIN_PAIR), k - LAG)
    own_tail(half)
    send_over(half)
    early = max(half - LAG, 0) + 1
    ring_step((TWIN, TWIN_PAIR), early)

    lane = lax.broadcasted_iota(jnp.int32, (8, 128), 1) // ROWS

    def gather_taps(p):
        def step(g, carry):
            lanes = pl.ds(pl.multiple_of(g * 128, 128), 128)
            tiles = [G[p, e % 2, 2 * g + e // 4, (e // 2) % 2, EARLY - 1] for e in range(8)]
            for q in range(8):
                row = jnp.zeros((8, 128), F32)
                for e in range(8):
                    shift = ((e - q) % 8) * ROWS
                    moved = pltpu.roll(tiles[e], shift, 1) if shift else tiles[e]
                    row = jnp.where(lane == e, moved, row)
                taps[p, q, :, lanes] = row
            return carry

        lax.fori_loop(0, T, step, 0)

    gather_taps(0)
    for c in local[1:]:
        c.wait()

    @pl.when(sec == 0)
    def _():
        for c in stems_zero:
            c.wait()

    @pl.when(sec == 1)
    def _():
        for c in stems_one:
            c.wait()

    col = lax.broadcasted_iota(jnp.int32, (1, GRID, KC), 1)

    def depthwise(v, p, b, kc, acts):
        def tap(t):
            n = 9 * b + t
            return taps[p, n % 8, n // 8:n // 8 + 1, kc * KC:(kc + 1) * KC].reshape(1, 1, KC)

        v = jnp.maximum(v.reshape(GRID, GRID, KC), 0.0)
        left, right = pltpu.roll(v, 1, 1), pltpu.roll(v, GRID - 1, 1)
        rows = []
        for i in range(3):
            kl = jnp.where(col == 0, 0.0, jnp.broadcast_to(tap(3 * i), (1, GRID, KC)))
            kr = jnp.where(col == GRID - 1, 0.0, jnp.broadcast_to(tap(3 * i + 2), (1, GRID, KC)))
            rows.append(left * kl + v * tap(3 * i + 1) + right * kr)
        zero = jnp.zeros((1, GRID, KC), F32)
        total = (jnp.concatenate([zero, rows[0][:GRID - 1]], 0) + rows[1]
                 + jnp.concatenate([rows[2][1:], zero], 0)).reshape(PIX, KC)
        hi = total.astype(BF16)
        lo = (total - hi.astype(F32)).astype(BF16)
        acts[:, kc * KC:(kc + 1) * KC] = hi
        acts[:, C + kc * KC:C + (kc + 1) * KC] = lo
        acts[:, 2 * C + kc * KC:2 * C + (kc + 1) * KC] = hi

    part = lambda nc: slice(nc * KC, (nc + 1) * KC)
    span = lambda nc: pl.ds(nc * KC, KC)

    def landed(m, nc):
        r = BUF.at[m, :, span(nc)]
        remote(r, r, mssem.at[m, nc], mrsem.at[m, nc], at(prv)).wait_recv()

    def pass_on(t, m, nc, dev):
        return remote(BUF.at[8 + t, :, span(nc)], BUF.at[m, :, span(nc)], mssem.at[m, nc], mrsem.at[m, nc], dev)

    up0 = lambda nc: pass_on(0, 4 - odd, nc, at(nxt2))
    up1 = lambda nc: pass_on(1, 5, nc, at(nxt2))
    up2 = lambda nc: pass_on(2, 7, nc, at(nxt))
    home = remote(BUF.at[9], OUT.at[1], mssem.at[8, 0], mrsem.at[8, 0], there(dp))
    again = lambda nc: remote(OUT.at[1, :, span(nc)], BUF.at[6, :, span(nc)], mssem.at[6, nc], mrsem.at[6, nc], at(nxt2))
    aside = remote(BUF.at[5, :, span(1)], BUF.at[6, :, span(1)], mssem.at[8, 1], mrsem.at[6, 1], there(dp))

    def cell(t, p):
        ear = jnp.where(t == 0, 0, jnp.where(t == 1, 1 + odd, jnp.where(t == 2, 4 - odd, 6)))
        new = jnp.where(t == 0, 1, jnp.where(t == 1, 8 - 5 * odd, jnp.where(t == 2, 5 + 4 * odd, 7)))

        def product(acts, b, nc):
            return jnp.dot(acts[...], W3[4 * p + b, :, nc * KC:(nc + 1) * KC], preferred_element_type=F32)

        @pl.when((t == 1) & (odd == 1) & (sec > 1))
        def _():
            r = BUF.at[2]
            remote(r, r, mssem.at[2, 0], mrsem.at[2, 0], at(prv2)).wait_recv()

        @pl.when((t == 2) & (sec < 2))
        def _():
            home.wait_recv()

        @pl.when((t == 2) & (odd == 0) & (sec > 1))
        def _():
            landed(4, 0)
            landed(4, 1)

        @pl.when((t == 3) & (sec > 1))
        def _():
            landed(6, 0)
            landed(6, 1)

        for kc in (0, 1):
            depthwise(BUF[ear, :, part(kc)], p, 1, kc, B3)
        for nc in (0, 1):
            first[:, part(nc)] = product(B3, 1, nc)
        for kc in (0, 1):
            @pl.when((t == 1) & (odd == 1) & (sec > 1))
            def _():
                landed(3, kc)

            @pl.when((t == 2) & (odd == 0) & (sec > 1))
            def _():
                landed(5, kc)
                if kc == 1:
                    aside.start()

            @pl.when((t == 3) & (sec > 0))
            def _():
                landed(7, kc)

            depthwise(BUF[new, :, part(kc)], p, 0, kc, A3)
        for nc in (0, 1):
            first[:, part(nc)] += product(A3, 0, nc)
        for kc in (0, 1):
            depthwise(first[:, part(kc)], p, 2, kc, B3)
        for nc in (0, 1):
            second[:, part(nc)] = product(B3, 2, nc) + BUF[new, :, part(nc)]
        for kc in (0, 1):
            depthwise(second[:, part(kc)], p, 3, kc, A3)
        for nc in (0, 1):
            v = product(A3, 3, nc) + first[:, part(nc)]
            BUF[8 + t, :, part(nc)] = v

            @pl.when(t != 1)
            def _():
                OUT[t, :, part(nc)] = v

            @pl.when((t == 0) & (sec < S - 2))
            def _():
                up0(nc).start()

            @pl.when((t == 1) & (odd == 0) & (sec < S - 2))
            def _():
                up1(nc).start()

            if nc == 0:
                @pl.when(t == 2)
                def _():
                    home.wait_send()

            @pl.when((t == 2) & (sec < S - 1))
            def _():
                up2(nc).start()

        @pl.when(t == 1)
        def _():
            home.start()

        @pl.when((t == 2) & (sec > 1))
        def _():
            home.wait_recv()

        @pl.when((t == 2) & (sec < S - 2))
        def _():
            again(0).start()

        @pl.when((t == 2) & (odd == 0) & (sec < S - 2))
        def _():
            again(1).start()

    cell(jnp.int32(0), 0)

    for k in range(early + 1, half + 1):
        ring_step((TWIN, TWIN_PAIR), k)
    for k in range(half + 1):
        twin_tail(k)
    for k in range(half + 1):
        from_core(1, k)
    gather_taps(1)

    def tick(t, carry):
        cell(t, jnp.where(t == 1, 1, 0))
        return carry

    lax.fori_loop(1, TICKS, tick, 0)

    for c in sent:
        c.wait_send()

    @pl.when((odd == 1) & (sec < S - 2))
    def _():
        old_copy.wait_send()

    @pl.when(sec < S - 2)
    def _():
        for nc in (0, 1):
            up0(nc).wait_send()
        again(0).wait_send()

    @pl.when((odd == 0) & (sec > 1))
    def _():
        aside.wait_send()

    @pl.when((odd == 0) & (sec < S - 2))
    def _():
        again(1).wait_send()
        for nc in (0, 1):
            up1(nc).wait_send()

    @pl.when(sec < S - 1)
    def _():
        for nc in (0, 1):
            up2(nc).wait_send()


def body(S, Y, pend, stem, spatial, mixing):
    C = mixing.shape[-1]
    T = C // 128
    pend = pend.reshape(2, PIX, C)
    stem = stem.reshape(TICKS - 1, PIX, C)
    flat = jnp.pad(spatial.reshape(36, ROWS), ((0, 28), (0, 0))).reshape(1, 8, 128)
    tiles = mixing.reshape(4, 2, 8, T, 128).transpose(0, 1, 3, 2, 4).reshape(8 * T, 8, 128)
    blk = jnp.concatenate([tiles[:4 * T], flat, tiles[4 * T:]], 0)
    dma = pltpu.SemaphoreType.DMA
    any_ = pl.BlockSpec(memory_space=pl.ANY)
    half = Y // 2
    out = pl.pallas_call(
        functools.partial(kernel, S, Y, C),
        out_shape=jax.ShapeDtypeStruct((TICKS, PIX, C), F32),
        in_specs=[any_] * 3,
        out_specs=pl.BlockSpec(memory_space=pltpu.VMEM),
        scratch_shapes=[
            pltpu.VMEM((2, 2, Y, 2, 8 * T + 1, 8, 128), F32),
            pltpu.VMEM((8, 3 * C, C), BF16),
            pltpu.VMEM((PIX, 3 * C), BF16),
            pltpu.VMEM((PIX, 3 * C), BF16),
            pltpu.VMEM((2, 8, 8, C), F32),
            pltpu.VMEM((12, PIX, C), F32),
            pltpu.VMEM((PIX, C), F32),
            pltpu.VMEM((PIX, C), F32),
            dma((13,)),
            dma((2, 5, half)),
            dma((2, 5, half)),
            dma((Y + 1,)),
            dma((Y + 1,)),
            dma((2, Y + 1)),
            dma((2, Y + 1)),
            dma((8, Y)),
            dma((8, Y)),
            dma((9, 2)),
            dma((9, 2)),
        ],
        compiler_params=pltpu.CompilerParams(collective_id=0, has_side_effects=True, vmem_limit_bytes=38 << 20),
        name="relay",
    )(pend, stem, blk)
    return out.reshape(1, TICKS, 1, GRID, GRID, C)


def solution(mesh):
    S, D = mesh.shape["section"], mesh.shape["dp"]
    placed = (
        P("section", None, "dp", None, None, None),
        P(None, "dp", None, None, None),
        P("section", None, None, "dp"),
        P("section", None, "dp", None),
    )
    return jax.shard_map(
        functools.partial(body, S, D // 4),
        mesh=mesh,
        in_specs=placed,
        out_specs=P("section", None, "dp", None, None, None),
        check_vma=False,
    )
```

```python
import functools

import jax
import jax.numpy as jnp
from jax import lax
from jax.experimental import pallas as pl
from jax.experimental.pallas import tpu as pltpu
from jax.sharding import PartitionSpec as P

MESH = pl.DeviceIdType.MESH
F32, BF16 = jnp.float32, jnp.bfloat16
GRID = 16
PIX = GRID * GRID
TICKS = 4
ROWS = 16
OWN, PAIR, LATE, TWIN, TWIN_PAIR = range(5)


def kernel(S, Y, C, pend, stem, blk, OUT, G, W3, A3, B3, taps, BUF, first, second,
           lsem, ssem, rsem, xssem, xsem, ossem, orsem, cssem, csem, mssem, mrsem):
    D = Y * 4
    T = C // 128
    EARLY, ALL = 4 * T + 1, 8 * T + 1
    KC = C // 2
    half = Y // 2
    sec, dp = lax.axis_index("section"), lax.axis_index("dp")
    odd = lax.rem(sec, 2)
    y, xl, core = dp // 4, lax.rem(dp // 2, 2), lax.rem(dp, 2)
    yup, ydn = lax.rem(dp + 4, D), lax.rem(dp + D - 4, D)
    xpair, cpair = dp + 2 - 4 * xl, dp + 1 - 2 * core
    twin = sec + 1 - 2 * odd
    here = lambda d: {"section": sec, "dp": d}
    at = lambda s: {"section": s, "dp": dp}
    there = lambda d: {"section": twin, "dp": d}
    nxt, nxt2 = lax.rem(sec + 1, S), lax.rem(sec + 2, S)
    prv, prv2 = lax.rem(sec + S - 1, S), lax.rem(sec + S - 2, S)

    local = [
        pltpu.make_async_copy(blk, G.at[0, core, y, xl], lsem.at[0]),
        pltpu.make_async_copy(pend.at[0], BUF.at[0], lsem.at[1]),
        pltpu.make_async_copy(pend.at[1], BUF.at[1], lsem.at[2]),
    ]
    for c in local:
        c.start()
    stems_zero = [pltpu.make_async_copy(stem.at[n], BUF.at[m], lsem.at[m]) for n, m in ((1, 4), (1, 5), (2, 6), (2, 7))]
    stems_one = [pltpu.make_async_copy(stem.at[n], BUF.at[m], lsem.at[m + 6]) for n, m in ((0, 2), (0, 3), (1, 6))]

    @pl.when(sec == 0)
    def _():
        for c in stems_zero:
            c.start()

    @pl.when(sec == 1)
    def _():
        for c in stems_one:
            c.start()

    barrier = pltpu.get_barrier_semaphore()
    partners = (here(yup), here(ydn), here(xpair), here(cpair), there(dp), there(xpair), at(nxt), at(prv), at(nxt2), at(prv2))
    for d in partners:
        pl.semaphore_signal(barrier, inc=1, device_id=d, device_id_type=MESH)
    pl.semaphore_wait(barrier, len(partners))
    local[0].wait()

    sent = []

    def remote(src, dst, s, r, dev):
        return pltpu.make_async_remote_copy(src_ref=src, dst_ref=dst, send_sem=s, recv_sem=r,
                                            device_id=dev, device_id_type=MESH)

    def send(c):
        c.start()
        sent.append(c)

    def piece(p, cc, yy, xx, late):
        lo, n = (EARLY, ALL - EARLY) if late else (0, EARLY)
        return G.at[p, cc, yy, xx, pl.ds(lo, n)]

    def column(stream):
        return xl if stream in (OWN, LATE, TWIN) else 1 - xl

    def place(way, k):
        return lax.rem(y + Y - k, Y) if way == 0 else lax.rem(y + k, Y)

    def ring_piece(stream, yy):
        return piece(1 if stream >= TWIN else 0, core, yy, column(stream), stream == LATE)

    def ring(way, stream, k):
        p = ring_piece(stream, place(way, k - 1))
        return remote(p, p, ssem.at[way, stream, k - 1], rsem.at[way, stream, k - 1], here(yup if way == 0 else ydn))

    def carried(way, stream, k):
        return k < half or (k == half and way == (1 if stream in (PAIR, TWIN_PAIR) else 0))

    def arrived(way, stream, k):
        yy = place(way, k)
        p = ring_piece(stream, yy)
        remote(p, p, ssem.at[way, stream, k - 1], rsem.at[way, stream, k - 1], here(ydn)).wait_recv()
        return yy

    def slot(way, k):
        return 0 if k == 0 else (k if way == 0 else Y - k)

    def cross(way, k):
        p = piece(0, core, place(way, k), xl, True)
        return remote(p, p, xssem.at[slot(way, k)], xsem.at[slot(way, k)], here(xpair))

    def crossed(way, k):
        p = piece(0, core, place(way, k), 1 - xl, True)
        remote(p, p, xssem.at[slot(way, k)], xsem.at[slot(way, k)], here(xpair)).wait_recv()

    def over(far, yy, late, n):
        return remote(piece(0, core, yy, xl, late), piece(1, core, yy, xl, late), ossem.at[far, n], orsem.at[far, n],
                      there(xpair if far else dp))

    def came_over(far, yy, late, n):
        p = piece(1, core, yy, 1 - xl if far else xl, late)
        remote(p, p, ossem.at[far, n], orsem.at[far, n], there(dp)).wait_recv()

    def share(p, yy, other, late, n):
        q, m = piece(p, core, yy, 1 - xl if other else xl, late), 4 * p + 2 * other + late
        send(remote(q, q, cssem.at[m, n], csem.at[m, n], here(cpair)))

    def shared(p, yy, other, late, n):
        q, m = piece(p, 1 - core, yy, 1 - xl if other else xl, late), 4 * p + 2 * other + late
        remote(q, q, cssem.at[m, n], csem.at[m, n], here(cpair)).wait_recv()

    def split(p, cc, yy, xx, late):
        row = pl.multiple_of(((yy * 2 + xx) * 2 + cc) * ROWS, ROWS)
        base = EARLY if late else 0

        def step(m, carry):
            b = 4 * p + (2 if late else 0) + m
            for j in range(T):
                w = jnp.concatenate([G[p, cc, yy, xx, base + m * 2 * T + j], G[p, cc, yy, xx, base + m * 2 * T + T + j]], 0)
                hi = w.astype(BF16)
                lo = (w - hi.astype(F32)).astype(BF16)
                lanes = slice(128 * j, 128 * j + 128)
                W3[b, pl.ds(row, ROWS), lanes] = hi
                W3[b, pl.ds(pl.multiple_of(C + row, ROWS), ROWS), lanes] = hi
                W3[b, pl.ds(pl.multiple_of(2 * C + row, ROWS), ROWS), lanes] = lo
            return carry

        lax.fori_loop(0, 2, step, 0)

    def both(k):
        return (0,) if k in (0, half) else (0, 1)

    def from_core(p, k):
        for way in both(k):
            yy = place(way, k)
            for other in (0, 1):
                for late in (0, 1):
                    shared(p, yy, other, late, slot(way, k))
                    split(p, 1 - core, yy, 1 - xl if other else xl, late)

    def ring_step(streams, k):
        got = []
        for stream in streams:
            for way in (0, 1):
                if not carried(way, stream, k):
                    continue
                yy = arrived(way, stream, k)
                if carried(way, stream, k + 1):
                    send(ring(way, stream, k + 1))
                n = slot(way, k)
                if stream == LATE:
                    send(cross(way, k))
                p = 1 if stream >= TWIN else 0
                share(p, yy, 1 if stream in (PAIR, TWIN_PAIR) else 0, 1 if stream == LATE else 0, n)
                got.append((p, yy, column(stream), stream == LATE))
        for p, yy, xx, late in got:
            split(p, core, yy, xx, late)

    def own_tail(k):
        for way in both(k):
            crossed(way, k)
            share(0, place(way, k), 1, 1, slot(way, k))
            split(0, core, place(way, k), 1 - xl, True)
        from_core(0, k)

    def send_over(k):
        for way in both(k):
            for far in (0, 1):
                send(over(far, place(way, k), True, slot(way, k)))

    def twin_tail(k):
        for way in both(k):
            for far in (0, 1):
                yy = place(way, k)
                came_over(far, yy, True, slot(way, k))
                share(1, yy, far, 1, slot(way, k))
                split(1, core, yy, 1 - xl if far else xl, True)

    own = piece(0, core, y, xl, False)
    send(remote(own, own, xssem.at[Y], xsem.at[Y], here(xpair)))
    for stream in (OWN, LATE):
        for way in (0, 1):
            if carried(way, stream, 1):
                send(ring(way, stream, 1))
    send(cross(0, 0))
    share(0, y, 0, 0, 0)
    share(0, y, 0, 1, 0)
    for far in (0, 1):
        send(over(far, y, False, Y))
    old_copy = remote(pend.at[1], BUF.at[2], mssem.at[2, 0], mrsem.at[2, 0], at(nxt2))

    @pl.when((odd == 1) & (sec < S - 2))
    def _():
        old_copy.start()

    split(0, core, y, xl, False)
    split(0, core, y, xl, True)
    other_own = piece(0, core, y, 1 - xl, False)
    remote(other_own, other_own, xssem.at[Y], xsem.at[Y], here(xpair)).wait_recv()
    for way in (0, 1):
        if carried(way, PAIR, 1):
            send(ring(way, PAIR, 1))
    share(0, y, 1, 0, 0)
    split(0, core, y, 1 - xl, False)

    def start_twin():
        for far in (0, 1):
            came_over(far, y, False, Y)
            for way in (0, 1):
                stream = TWIN_PAIR if far else TWIN
                if carried(way, stream, 1):
                    send(ring(way, stream, 1))
            share(1, y, far, 0, 0)
            split(1, core, y, 1 - xl if far else xl, False)

    LAG = 2
    for k in range(1, half + 1):
        ring_step((LATE, OWN, PAIR), k)
        own_tail(k - 1)
        send_over(k - 1)
        if k == min(LAG, half):
            start_twin()
        if k > LAG:
            ring_step((TWIN, TWIN_PAIR), k - LAG)
    own_tail(half)
    send_over(half)

    lane = lax.broadcasted_iota(jnp.int32, (8, 128), 1) // ROWS

    def gather_taps(p):
        def step(g, carry):
            lanes = pl.ds(pl.multiple_of(g * 128, 128), 128)
            tiles = [G[p, e % 2, 2 * g + e // 4, (e // 2) % 2, EARLY - 1] for e in range(8)]
            for q in range(8):
                row = jnp.zeros((8, 128), F32)
                for e in range(8):
                    shift = ((e - q) % 8) * ROWS
                    moved = pltpu.roll(tiles[e], shift, 1) if shift else tiles[e]
                    row = jnp.where(lane == e, moved, row)
                taps[p, q, :, lanes] = row
            return carry

        lax.fori_loop(0, T, step, 0)

    gather_taps(0)
    for c in local[1:]:
        c.wait()

    @pl.when(sec == 0)
    def _():
        for c in stems_zero:
            c.wait()

    @pl.when(sec == 1)
    def _():
        for c in stems_one:
            c.wait()

    col = lax.broadcasted_iota(jnp.int32, (1, GRID, KC), 1)

    def depthwise(v, p, b, kc, acts):
        def tap(t):
            n = 9 * b + t
            return taps[p, n % 8, n // 8:n // 8 + 1, kc * KC:(kc + 1) * KC].reshape(1, 1, KC)

        v = jnp.maximum(v.reshape(GRID, GRID, KC), 0.0)
        left, right = pltpu.roll(v, 1, 1), pltpu.roll(v, GRID - 1, 1)
        rows = []
        for i in range(3):
            kl = jnp.where(col == 0, 0.0, jnp.broadcast_to(tap(3 * i), (1, GRID, KC)))
            kr = jnp.where(col == GRID - 1, 0.0, jnp.broadcast_to(tap(3 * i + 2), (1, GRID, KC)))
            rows.append(left * kl + v * tap(3 * i + 1) + right * kr)
        zero = jnp.zeros((1, GRID, KC), F32)
        total = (jnp.concatenate([zero, rows[0][:GRID - 1]], 0) + rows[1]
                 + jnp.concatenate([rows[2][1:], zero], 0)).reshape(PIX, KC)
        hi = total.astype(BF16)
        lo = (total - hi.astype(F32)).astype(BF16)
        acts[:, kc * KC:(kc + 1) * KC] = hi
        acts[:, C + kc * KC:C + (kc + 1) * KC] = lo
        acts[:, 2 * C + kc * KC:2 * C + (kc + 1) * KC] = hi

    part = lambda nc: slice(nc * KC, (nc + 1) * KC)
    span = lambda nc: pl.ds(nc * KC, KC)

    def landed(m, nc):
        r = BUF.at[m, :, span(nc)]
        remote(r, r, mssem.at[m, nc], mrsem.at[m, nc], at(prv)).wait_recv()

    def pass_on(t, m, nc, dev):
        return remote(BUF.at[8 + t, :, span(nc)], BUF.at[m, :, span(nc)], mssem.at[m, nc], mrsem.at[m, nc], dev)

    up0 = lambda nc: pass_on(0, 4 - odd, nc, at(nxt2))
    up1 = lambda nc: pass_on(1, 5, nc, at(nxt2))
    up2 = lambda nc: pass_on(2, 7, nc, at(nxt))
    home = remote(BUF.at[9], OUT.at[1], mssem.at[8, 0], mrsem.at[8, 0], there(dp))
    again = lambda nc: remote(OUT.at[1, :, span(nc)], BUF.at[6, :, span(nc)], mssem.at[6, nc], mrsem.at[6, nc], at(nxt2))
    aside = remote(BUF.at[5, :, span(1)], BUF.at[6, :, span(1)], mssem.at[8, 1], mrsem.at[6, 1], there(dp))

    def cell(t, p):
        ear = jnp.where(t == 0, 0, jnp.where(t == 1, 1 + odd, jnp.where(t == 2, 4 - odd, 6)))
        new = jnp.where(t == 0, 1, jnp.where(t == 1, 8 - 5 * odd, jnp.where(t == 2, 5 + 4 * odd, 7)))

        def product(acts, b, nc):
            return jnp.dot(acts[...], W3[4 * p + b, :, nc * KC:(nc + 1) * KC], preferred_element_type=F32)

        @pl.when((t == 1) & (odd == 1) & (sec > 1))
        def _():
            r = BUF.at[2]
            remote(r, r, mssem.at[2, 0], mrsem.at[2, 0], at(prv2)).wait_recv()

        @pl.when((t == 2) & (sec < 2))
        def _():
            home.wait_recv()

        @pl.when((t == 2) & (odd == 0) & (sec > 1))
        def _():
            landed(4, 0)
            landed(4, 1)

        @pl.when((t == 3) & (sec > 1))
        def _():
            landed(6, 0)
            landed(6, 1)

        for kc in (0, 1):
            depthwise(BUF[ear, :, part(kc)], p, 1, kc, B3)
        for nc in (0, 1):
            first[:, part(nc)] = product(B3, 1, nc)
        for kc in (0, 1):
            @pl.when((t == 1) & (odd == 1) & (sec > 1))
            def _():
                landed(3, kc)

            @pl.when((t == 2) & (odd == 0) & (sec > 1))
            def _():
                landed(5, kc)
                if kc == 1:
                    aside.start()

            @pl.when((t == 3) & (sec > 0))
            def _():
                landed(7, kc)

            depthwise(BUF[new, :, part(kc)], p, 0, kc, A3)
        for nc in (0, 1):
            first[:, part(nc)] += product(A3, 0, nc)
        for kc in (0, 1):
            depthwise(first[:, part(kc)], p, 2, kc, B3)
        for nc in (0, 1):
            second[:, part(nc)] = product(B3, 2, nc) + BUF[new, :, part(nc)]
        for kc in (0, 1):
            depthwise(second[:, part(kc)], p, 3, kc, A3)
        for nc in (0, 1):
            v = product(A3, 3, nc) + first[:, part(nc)]
            BUF[8 + t, :, part(nc)] = v

            @pl.when(t != 1)
            def _():
                OUT[t, :, part(nc)] = v

            @pl.when((t == 0) & (sec < S - 2))
            def _():
                up0(nc).start()

            @pl.when((t == 1) & (odd == 0) & (sec < S - 2))
            def _():
                up1(nc).start()

            if nc == 0:
                @pl.when(t == 2)
                def _():
                    home.wait_send()

            @pl.when((t == 2) & (sec < S - 1))
            def _():
                up2(nc).start()

        @pl.when(t == 1)
        def _():
            home.start()

        @pl.when((t == 2) & (sec > 1))
        def _():
            home.wait_recv()

        @pl.when((t == 2) & (sec < S - 2))
        def _():
            again(0).start()

        @pl.when((t == 2) & (odd == 0) & (sec < S - 2))
        def _():
            again(1).start()

    cell(jnp.int32(0), 0)

    done = max(half - LAG, 0)
    for k in range(done + 1, half):
        ring_step((TWIN, TWIN_PAIR), k)
    for k in range(done + 1):
        twin_tail(k)
    for k in range(done + 1):
        from_core(1, k)
    if done < half:
        ring_step((TWIN, TWIN_PAIR), half)
    for k in range(done + 1, half + 1):
        twin_tail(k)
    for k in range(done + 1, half + 1):
        from_core(1, k)
    gather_taps(1)

    def tick(t, carry):
        cell(t, jnp.where(t == 1, 1, 0))
        return carry

    lax.fori_loop(1, TICKS, tick, 0)

    for c in sent:
        c.wait_send()

    @pl.when((odd == 1) & (sec < S - 2))
    def _():
        old_copy.wait_send()

    @pl.when(sec < S - 2)
    def _():
        for nc in (0, 1):
            up0(nc).wait_send()
        again(0).wait_send()

    @pl.when((odd == 0) & (sec > 1))
    def _():
        aside.wait_send()

    @pl.when((odd == 0) & (sec < S - 2))
    def _():
        again(1).wait_send()
        for nc in (0, 1):
            up1(nc).wait_send()

    @pl.when(sec < S - 1)
    def _():
        for nc in (0, 1):
            up2(nc).wait_send()


def body(S, Y, pend, stem, spatial, mixing):
    C = mixing.shape[-1]
    T = C // 128
    pend = pend.reshape(2, PIX, C)
    stem = stem.reshape(TICKS - 1, PIX, C)
    flat = jnp.pad(spatial.reshape(36, ROWS), ((0, 28), (0, 0))).reshape(1, 8, 128)
    tiles = mixing.reshape(4, 2, 8, T, 128).transpose(0, 1, 3, 2, 4).reshape(8 * T, 8, 128)
    blk = jnp.concatenate([tiles[:4 * T], flat, tiles[4 * T:]], 0)
    dma = pltpu.SemaphoreType.DMA
    any_ = pl.BlockSpec(memory_space=pl.ANY)
    half = Y // 2
    out = pl.pallas_call(
        functools.partial(kernel, S, Y, C),
        out_shape=jax.ShapeDtypeStruct((TICKS, PIX, C), F32),
        in_specs=[any_] * 3,
        out_specs=pl.BlockSpec(memory_space=pltpu.VMEM),
        scratch_shapes=[
            pltpu.VMEM((2, 2, Y, 2, 8 * T + 1, 8, 128), F32),
            pltpu.VMEM((8, 3 * C, C), BF16),
            pltpu.VMEM((PIX, 3 * C), BF16),
            pltpu.VMEM((PIX, 3 * C), BF16),
            pltpu.VMEM((2, 8, 8, C), F32),
            pltpu.VMEM((12, PIX, C), F32),
            pltpu.VMEM((PIX, C), F32),
            pltpu.VMEM((PIX, C), F32),
            dma((13,)),
            dma((2, 5, half)),
            dma((2, 5, half)),
            dma((Y + 1,)),
            dma((Y + 1,)),
            dma((2, Y + 1)),
            dma((2, Y + 1)),
            dma((8, Y)),
            dma((8, Y)),
            dma((9, 2)),
            dma((9, 2)),
        ],
        compiler_params=pltpu.CompilerParams(collective_id=0, has_side_effects=True, vmem_limit_bytes=38 << 20),
        name="relay",
    )(pend, stem, blk)
    return out.reshape(1, TICKS, 1, GRID, GRID, C)


def solution(mesh):
    S, D = mesh.shape["section"], mesh.shape["dp"]
    placed = (
        P("section", None, "dp", None, None, None),
        P(None, "dp", None, None, None),
        P("section", None, None, "dp"),
        P("section", None, "dp", None),
    )
    return jax.shard_map(
        functools.partial(body, S, D // 4),
        mesh=mesh,
        in_specs=placed,
        out_specs=P("section", None, "dp", None, None, None),
        check_vma=False,
    )
```
